512 devices in a mesh: tok: 128 (over y, z_hi, x), tp: 4 (over z_lo, core).
Axes of the slice: x: 4, y: 8, z: 8 (z_hi: 4, z_lo: 2; z = z_hi * 2 + z_lo), core: 2. Of those that a mesh axis runs over, the one named last changes fastest.
Arguments:
- tokens: bfloat16 [131072, 1024], P('tok', 'tp'), may hold values from -6 to 6
- mix_weights: bfloat16 [10, 2, 2, 128, 128], replicated, may hold values from -0.375 to 0.375
- proj_weight: bfloat16 [1024, 2048], P('tp'), may hold values from -0.1875 to 0.1875
- pool_map: int32 [131072], P('tok'), may hold values from 0 to 16383, as said below
- out_cot: bfloat16 [16384, 2048], P('tok', 'tp'), may hold values from -24 to 24
Outputs:
- projected: bfloat16 [16384, 2048], P('tok', 'tp')
- token_grad: bfloat16 [131072, 1024], P('tok', 'tp')
- proj_grad: float32 [2048, 1024], P('tok', 'tp')
The draws below stay inside these ranges and needn't reach their ends.
Inputs may be any that keep to these rules, and one draw needn't show every extreme that they name: `pool_map`: token t names one of the 128 pooled tokens of its own block of 1024 tokens, numbers (t // 1024) * 128 onward; every pooled token is named by at least one token.
All inputs are finite; a program needn't handle non-finite values.
Results may differ from the reference program's by a relative error of at most 0.017.
Values may be sent and summed in bfloat16 or wider, within the bound.
A program may use at most 64 MiB of HBM per device.

```python
import math
import jax
import jax.numpy as jnp
from jax import lax

D = 1024
E = 2048
BLK = 128
SECTIONS = 10
TOK_DEV = 1024
POOL_DEV = 128
TOKENS = 131072
POOLED = 16384


def draw_pool_map(key, part):
    blocks = TOKENS // TOK_DEV
    rank_keys = jax.random.split(jax.random.fold_in(key, 11), blocks)
    ranks = jax.vmap(lambda sub_key: jax.random.permutation(sub_key, TOK_DEV))(rank_keys)
    extra_ids = jax.random.randint(jax.random.fold_in(key, 12), (blocks, TOK_DEV), 0, POOL_DEV)
    local_ids = jnp.where(ranks < POOL_DEV, ranks, extra_ids)
    offsets = jnp.arange(blocks, dtype=jnp.int32)[:, None] * POOL_DEV
    return (local_ids + offsets).astype(jnp.int32).reshape(TOKENS)


def with_spikes(drawn, key, source, target, parts, factor):
    owner, partner = [(jnp.arange(drawn.shape[dim]) // (drawn.shape[dim] // parts)).reshape([-1 if axis == dim else 1 for axis in range(drawn.ndim)]) for dim in (source, target)]
    chosen = jax.random.permutation(key, parts)[partner]
    strong = (owner == chosen) | (owner == (partner + parts // 2) % parts)
    return jnp.where(strong, factor * drawn, drawn)


def shard_levels(key, extent, cuts, least, high):
    def one(dim, shards_of):
        draws = jax.random.uniform(jax.random.fold_in(jax.random.fold_in(key, 6), dim), (shards_of,), jnp.float32, least / len(cuts), high / len(cuts))
        return jnp.repeat(jnp.exp(draws), extent[dim] // shards_of).reshape((-1,) + (1,) * (len(extent) - dim - 1))

    factor_of = one(*cuts[0])
    for cut in cuts[1:]:
        factor_of = factor_of * one(*cut)
    return factor_of


def centred(rng, shape, deviation, reach, shards=(), kind=jnp.bfloat16):
    result = jax.random.normal(rng, shape, jnp.float32) * deviation
    if len(shards) > 0:
        result = shard_levels(rng, shape, shards, -0.22, 0.18) * result
    return jnp.clip(result, min=-reach, max=reach).astype(kind)


def heavy_noise(rng, dims, scale, reach, cuts, heavy, kind=jnp.bfloat16):
    array = scale * jax.random.normal(rng, dims, jnp.float32)
    if cuts:
        array = array * shard_levels(rng, dims, cuts, -0.22, 0.18)
    return jnp.clip(with_spikes(array, jax.random.fold_in(rng, 3), *heavy), -reach, reach).astype(kind)


def setup_inputs(seed: int = 0) -> dict:
    arg_keys = jax.random.split(jax.random.key(seed), 6)
    return {
        "tokens": centred(arg_keys[0], (TOKENS, D), 1.0, 6.0, ((0, 128), (1, 4))),
        "mix_weights": centred(arg_keys[1], (SECTIONS, 2, 2, BLK, BLK), (2 * BLK) ** -0.5, 0.375),
        "proj_weight": centred(arg_keys[2], (D, E), D ** -0.5, 0.1875, ((0, 4),)),
        "pool_map": draw_pool_map(jax.random.fold_in(arg_keys[5], 71), 0),
        "out_cot": heavy_noise(arg_keys[4], (POOLED, E), 1.0, 24.0, ((0, 128), (1, 4)), (0, 1, 128, 5.5)),
    }


def contract(matrix, operand, backward):
    pattern = 'ji,...jf->...if' if backward else 'ij,...jf->...if'
    return jnp.einsum(pattern, matrix.astype(jnp.float32), operand.astype(jnp.float32))

def apply_section(source, section_mats, bit_index, backward):
    full_shape = source.shape
    nblocks = full_shape[0]
    paired = source.reshape((nblocks >> bit_index + 1, 2, 1 << bit_index) + full_shape[1:])
    lower_half = paired[:, 0]
    upper_half = paired[:, 1]
    if backward:
        new_lower = contract(section_mats[0, 0], lower_half, True) + contract(section_mats[1, 0], upper_half, True)
        new_upper = contract(section_mats[0, 1], lower_half, True) + contract(section_mats[1, 1], upper_half, True)
    else:
        new_lower = contract(section_mats[0, 0], lower_half, False) + contract(section_mats[0, 1], upper_half, False)
        new_upper = contract(section_mats[1, 0], lower_half, False) + contract(section_mats[1, 1], upper_half, False)
    joined = jnp.stack([new_lower.astype(jnp.bfloat16), new_upper.astype(jnp.bfloat16)], axis=1)
    return joined.reshape(full_shape)

def reference(tokens, mix_weights, proj_weight, pool_map, out_cot):
    token_count = tokens.shape[0]
    feat_width = tokens.shape[1]
    block_rows = mix_weights.shape[-1]
    section_count = mix_weights.shape[0]
    block_count = token_count // block_rows
    all_bits = block_count.bit_length() - 1
    section_bits = [section_id % all_bits for section_id in range(section_count)]

    def mix_tokens(source, backward):
        groups = source.reshape(token_count, feat_width // 128, 128).transpose(1, 0, 2)

        def mix_slab(slab):
            field_now = slab.reshape(block_count, block_rows, 128)
            section_order = list(range(section_count))
            if backward:
                section_order = section_order[::-1]
            for section_id in section_order:
                field_now = apply_section(field_now, mix_weights[section_id], section_bits[section_id], backward)
            return field_now.reshape(token_count, 128)
        mixed_groups = lax.map(mix_slab, groups)
        return mixed_groups.transpose(1, 0, 2).reshape(token_count, feat_width)
    mixed = mix_tokens(tokens, False)
    pooled_rows = out_cot.shape[0]
    group_sums = jax.ops.segment_sum(mixed.astype(jnp.float32), pool_map, num_segments=pooled_rows)
    counts = jax.ops.segment_sum(jnp.ones((token_count,), jnp.float32), pool_map, num_segments=pooled_rows)
    pooled = (group_sums / counts[:, None]).astype(jnp.bfloat16)
    projected = jnp.dot(pooled, proj_weight, preferred_element_type=jnp.float32).astype(jnp.bfloat16)
    d_pooled = jnp.dot(out_cot, proj_weight.T, preferred_element_type=jnp.float32)
    back_rows = jnp.take(d_pooled / counts[:, None], pool_map, axis=0).astype(jnp.bfloat16)
    token_grad = mix_tokens(back_rows, True)
    grad_scale = 1.0 / math.sqrt(pooled_rows)
    proj_grad = jnp.dot(out_cot.T, pooled, preferred_element_type=jnp.float32) * grad_scale
    return (projected, token_grad, proj_grad)
```

```python
import functools
import math

import jax
import jax.numpy as jnp
from jax import lax
from jax.experimental import pallas as pl
from jax.experimental.pallas import tpu as pltpu
from jax.sharding import PartitionSpec as P

MESH = pl.DeviceIdType.MESH
BLK = 128
NX = 4
NN = (((1,), (0,)), ((), ()))
NT = (((1,), (1,)), ((), ()))
F_IN, F_OUT, B_IN, B_OUT, COT, COTX, POOLX, PROJ, GRAD = range(9)


def mm(a, b, dims):
    return lax.dot_general(a, b, dims, preferred_element_type=jnp.float32)


def section_matrix(mixw, s):
    top = jnp.concatenate([mixw[s, 0, 0], mixw[s, 0, 1]], axis=1)
    low = jnp.concatenate([mixw[s, 1, 0], mixw[s, 1, 1]], axis=1)
    return jnp.concatenate([top, low], axis=0)


def wait_bytes(sem, ref):
    pltpu.make_async_copy(ref, ref, sem).wait()


def kernel(
    nt, ntp, tokens, mixw, pw, pmap, cot, projected, token_grad, proj_grad,
    xs, yt, xr, gs, ut, vt, onehot, cf, cx, pool, px, ps, pr, cs, cr, send, recv,
):
    me = lax.axis_index("tok")
    mytp = lax.axis_index("tp")
    feats = tokens.shape[1]
    blocks = tokens.shape[0] // BLK
    groups = nt // blocks
    frows = feats // groups
    npool = cot.shape[0]
    equart = cot.shape[1]
    others = nt // NX
    mex, mehi = lax.rem(me, NX), lax.div(me, NX)

    barrier = pltpu.get_barrier_semaphore()

    def greet(i, c):
        pl.semaphore_signal(barrier, inc=1, device_id={"tok": lax.rem(me + i, nt)}, device_id_type=MESH)
        return c

    lax.fori_loop(1, nt, greet, 0)
    for i in range(1, ntp):
        pl.semaphore_signal(barrier, inc=1, device_id={"tp": lax.rem(mytp + i, ntp)}, device_id_type=MESH)

    def exchange(kind, src, dst):
        def one(i, c):
            d = lax.rem(me + i, nt)
            pltpu.make_async_remote_copy(
                src_ref=src.at[d], dst_ref=dst.at[me], send_sem=send.at[kind], recv_sem=recv.at[kind],
                device_id={"tok": d}, device_id_type=MESH,
            ).start()
            return c

        pltpu.make_async_copy(src.at[me], dst.at[me], recv.at[kind]).start()
        lax.fori_loop(1, nt, one, 0)

    def load_block(ref, j):
        parts = [ref[g * blocks + j] for g in range(groups)]
        return jnp.concatenate(parts, axis=0) if groups > 1 else parts[0]

    def store_block(ref, j, value):
        for g in range(groups):
            ref[g * blocks + j] = value[g * frows : (g + 1) * frows]

    def local_pairs(bit):
        return [(j, j | (1 << bit)) for j in range(blocks) if not j & (1 << bit)]

    cf[mytp] = cot[...].astype(jnp.float32).T.astype(jnp.bfloat16)

    w = section_matrix(mixw, 0)
    for lo, hi in local_pairs(0):
        out = mm(w, tokens[lo * BLK : (hi + 1) * BLK], NN).T.astype(jnp.bfloat16)
        store_block(xs, lo, out[:, :BLK])
        store_block(xs, hi, out[:, BLK:])
    for bit in (1, 2):
        w = section_matrix(mixw, bit)
        for lo, hi in local_pairs(bit):
            pair = jnp.concatenate([load_block(xs, lo), load_block(xs, hi)], axis=1)
            out = mm(pair, w, NT).astype(jnp.bfloat16)
            store_block(xs, lo, out[:, :BLK])
            store_block(xs, hi, out[:, BLK:])

    pl.semaphore_wait(barrier, nt - 1 + ntp - 1)

    for i in range(1, ntp):
        d = lax.rem(mytp + i, ntp)
        pltpu.make_async_remote_copy(
            src_ref=cf.at[mytp], dst_ref=cf.at[mytp], send_sem=send.at[COT], recv_sem=recv.at[COT],
            device_id={"tp": d}, device_id_type=MESH,
        ).start()
    exchange(F_IN, xs, yt)

    pid = lax.broadcasted_iota(jnp.int32, (npool, BLK), 0) + me * npool
    for j in range(blocks):
        hit = pid == jnp.broadcast_to(pmap[j : j + 1, :], (npool, BLK))
        onehot[:, j * BLK : (j + 1) * BLK] = jnp.where(hit, 1.0, 0.0).astype(jnp.bfloat16)
    ones = jnp.ones((8, blocks * BLK), jnp.bfloat16)
    counts_row = mm(ones, onehot[...], NT)[0:1]
    counts_col = jnp.sum(onehot[...].astype(jnp.float32), axis=1, keepdims=True)

    wait_bytes(recv.at[COT], cf.at[pl.ds(0, ntp - 1)])
    dp = mm(pw[:, 0:equart], cf[0], NN)
    for i in range(1, ntp):
        dp = dp + mm(pw[:, i * equart : (i + 1) * equart], cf[i], NN)
    dp = (dp / counts_row).astype(jnp.bfloat16)
    for j in range(blocks):
        store_block(gs, j, mm(dp, onehot[:, j * BLK : (j + 1) * BLK], NN).astype(jnp.bfloat16))
    exchange(B_IN, gs, ut)

    for i in range(NX):
        dx = lax.rem(mex + i, NX)
        if i == 0:
            pltpu.make_async_copy(cf.at[dx], cx.at[mex], recv.at[COTX]).start()
        else:
            pltpu.make_async_remote_copy(
                src_ref=cf.at[dx], dst_ref=cx.at[mex], send_sem=send.at[COTX], recv_sem=recv.at[COTX],
                device_id={"tok": mehi * NX + dx}, device_id_type=MESH,
            ).start()

    def across(ref, bit, s, dims):
        w = section_matrix(mixw, s)
        stride = 1 << bit
        half = nt // 2
        run = min(16, half)

        def body(c, carry):
            if stride >= run:
                p = c * run
                lo = (p // stride) * (2 * stride) + p % stride
                lo = pl.multiple_of(lo, run)
                a = ref[pl.ds(lo, run)].reshape(run * frows, BLK)
                b = ref[pl.ds(lo + stride, run)].reshape(run * frows, BLK)
                out = mm(jnp.concatenate([a, b], axis=1), w, dims).astype(jnp.bfloat16)
                ref[pl.ds(lo, run)] = out[:, :BLK].reshape(run, frows, BLK)
                ref[pl.ds(lo + stride, run)] = out[:, BLK:].reshape(run, frows, BLK)
            else:
                base = c * 2 * run
                v = ref[pl.ds(base, 2 * run)].reshape(run // stride, 2, stride, frows, BLK)
                a = v[:, 0].reshape(run * frows, BLK)
                b = v[:, 1].reshape(run * frows, BLK)
                out = mm(jnp.concatenate([a, b], axis=1), w, dims).astype(jnp.bfloat16)
                a = out[:, :BLK].reshape(run // stride, 1, stride, frows, BLK)
                b = out[:, BLK:].reshape(run // stride, 1, stride, frows, BLK)
                ref[pl.ds(base, 2 * run)] = jnp.concatenate([a, b], axis=1).reshape(2 * run, frows, BLK)
            return carry

        lax.fori_loop(0, half // run, body, 0)

    bits = nt.bit_length() - 1
    wait_bytes(recv.at[F_IN], yt)
    for bit in range(bits):
        across(yt, bit, 3 + bit, NT)
    exchange(F_OUT, yt, xr)

    wait_bytes(recv.at[B_IN], ut)
    for bit in reversed(range(bits)):
        across(ut, bit, 3 + bit, NN)
    exchange(B_OUT, ut, vt)

    wait_bytes(recv.at[F_OUT], xr)
    total = mm(onehot[:, 0:BLK], load_block(xr, 0), NT)
    for j in range(1, blocks):
        total = total + mm(onehot[:, j * BLK : (j + 1) * BLK], load_block(xr, j), NT)
    pool[...] = (total / counts_col).astype(jnp.bfloat16)
    for i in range(NX):
        dx = lax.rem(mex + i, NX)
        if i == 0:
            pltpu.make_async_copy(pool, px.at[mex], recv.at[POOLX]).start()
        else:
            pltpu.make_async_remote_copy(
                src_ref=pool, dst_ref=px.at[mex], send_sem=send.at[POOLX], recv_sem=recv.at[POOLX],
                device_id={"tok": mehi * NX + dx}, device_id_type=MESH,
            ).start()
    for i in range(ntp):
        ps[i] = mm(pool[...], pw[:, i * equart : (i + 1) * equart], NN).astype(jnp.bfloat16)
    pltpu.make_async_copy(ps.at[mytp], pr.at[mytp], recv.at[PROJ]).start()
    for i in range(1, ntp):
        d = lax.rem(mytp + i, ntp)
        pltpu.make_async_remote_copy(
            src_ref=ps.at[d], dst_ref=pr.at[mytp], send_sem=send.at[PROJ], recv_sem=recv.at[PROJ],
            device_id={"tp": d}, device_id_type=MESH,
        ).start()

    wait_bytes(recv.at[COTX], cx)
    wait_bytes(recv.at[POOLX], px)
    erows = equart // others
    parts = min(4, others)
    half = equart // parts
    for r in range(parts):
        part = mm(cx[0, r * half : (r + 1) * half], px[0], NN)
        for i in range(1, NX):
            part = part + mm(cx[i, r * half : (r + 1) * half], px[i], NN)
        n = others // parts
        cs[r * n : (r + 1) * n] = part.astype(jnp.bfloat16).reshape(n, erows, feats)

    def give(i, c):
        b = lax.rem(mehi + i, others)
        d = mex * others + b

        @pl.when(d == me)
        def _():
            pltpu.make_async_copy(cs.at[b], cr.at[mehi], recv.at[GRAD]).start()

        @pl.when(d != me)
        def _():
            pltpu.make_async_remote_copy(
                src_ref=cs.at[b], dst_ref=cr.at[mehi], send_sem=send.at[GRAD], recv_sem=recv.at[GRAD],
                device_id={"tok": d}, device_id_type=MESH,
            ).start()

        return c

    lax.fori_loop(0, others, give, 0)

    wait_bytes(recv.at[B_OUT], vt)
    for bit in (2, 1):
        w = section_matrix(mixw, bit)
        for lo, hi in local_pairs(bit):
            pair = jnp.concatenate([load_block(vt, lo), load_block(vt, hi)], axis=1)
            out = mm(pair, w, NN).astype(jnp.bfloat16)
            store_block(vt, lo, out[:, :BLK])
            store_block(vt, hi, out[:, BLK:])
    w = section_matrix(mixw, 0)
    for lo, hi in local_pairs(0):
        pair = jnp.concatenate([load_block(vt, lo), load_block(vt, hi)], axis=1)
        token_grad[lo * BLK : (hi + 1) * BLK] = mm(pair, w, NN).T.astype(jnp.bfloat16)

    wait_bytes(recv.at[PROJ], pr)
    proj = pr[0].astype(jnp.float32)
    for i in range(1, ntp):
        proj = proj + pr[i].astype(jnp.float32)
    projected[...] = proj.astype(jnp.bfloat16)

    wait_bytes(recv.at[GRAD], cr)
    proj_grad[...] = jnp.sum(cr[...].astype(jnp.float32), axis=0) * (1.0 / math.sqrt(npool * nt))

    for kind, ref in ((F_IN, yt), (B_IN, ut), (F_OUT, xr), (B_OUT, vt)):
        wait_bytes(send.at[kind], ref.at[pl.ds(0, nt - 1)])
    wait_bytes(send.at[COT], cf.at[pl.ds(0, ntp - 1)])
    wait_bytes(send.at[PROJ], pr.at[pl.ds(0, ntp - 1)])
    wait_bytes(send.at[COTX], cx.at[pl.ds(0, NX - 1)])
    wait_bytes(send.at[POOLX], px.at[pl.ds(0, NX - 1)])
    mine = lax.div(me, others) == mex

    @pl.when(mine)
    def _():
        wait_bytes(send.at[GRAD], cr.at[pl.ds(0, others - 1)])

    @pl.when(jnp.logical_not(mine))
    def _():
        wait_bytes(send.at[GRAD], cr)


def shards(nt, ntp, tokens, mixw, pw, pool_map, cot):
    rows, feats = tokens.shape
    blocks = rows // BLK
    frows = feats * blocks // nt
    npool, equart = cot.shape
    others = nt // NX
    erows = equart // others
    bf = jnp.bfloat16
    tiles = pltpu.VMEM((nt, frows, BLK), bf)
    vmem = pl.BlockSpec(memory_space=pltpu.VMEM)
    return pl.pallas_call(
        functools.partial(kernel, nt, ntp),
        out_shape=(
            jax.ShapeDtypeStruct((npool, equart), bf),
            jax.ShapeDtypeStruct((rows, feats), bf),
            jax.ShapeDtypeStruct((erows, feats), jnp.float32),
        ),
        in_specs=[vmem] * 5,
        out_specs=(vmem,) * 3,
        scratch_shapes=[
            tiles, tiles, tiles, tiles, tiles, tiles,
            pltpu.VMEM((npool, rows), bf),
            pltpu.VMEM((ntp, equart, npool), bf),
            pltpu.VMEM((NX, equart, npool), bf),
            pltpu.VMEM((npool, feats), bf),
            pltpu.VMEM((NX, npool, feats), bf),
            pltpu.VMEM((ntp, npool, equart), bf),
            pltpu.VMEM((ntp, npool, equart), bf),
            pltpu.VMEM((others, erows, feats), bf),
            pltpu.VMEM((others, erows, feats), bf),
            pltpu.SemaphoreType.DMA((9,)),
            pltpu.SemaphoreType.DMA((9,)),
        ],
        compiler_params=pltpu.CompilerParams(collective_id=0, has_side_effects=True),
    )(tokens, mixw, pw, pool_map.reshape(blocks, BLK), cot)


def solution(mesh):
    nt, ntp = mesh.shape["tok"], mesh.shape["tp"]
    return jax.shard_map(
        functools.partial(shards, nt, ntp),
        mesh=mesh,
        in_specs=(P("tok", "tp"), P(), P("tp", None), P("tok"), P("tok", "tp")),
        out_specs=(P("tok", "tp"), P("tok", "tp"), P("tok", "tp")),
        check_vma=False,
    )
```

```python
import functools
import math

import jax
import jax.numpy as jnp
from jax import lax
from jax.experimental import pallas as pl
from jax.experimental.pallas import tpu as pltpu
from jax.sharding import PartitionSpec as P

MESH = pl.DeviceIdType.MESH
BLK = 128
NX = 4
NN = (((1,), (0,)), ((), ()))
NT = (((1,), (1,)), ((), ()))
F_IN, F_OUT, B_IN, B_OUT, COT, COTX, POOLX, PROJ, GRAD, COTZ, PROJZ = range(11)


def mm(a, b, dims):
    return lax.dot_general(a, b, dims, preferred_element_type=jnp.float32)


def section_matrix(mixw, s):
    top = jnp.concatenate([mixw[s, 0, 0], mixw[s, 0, 1]], axis=1)
    low = jnp.concatenate([mixw[s, 1, 0], mixw[s, 1, 1]], axis=1)
    return jnp.concatenate([top, low], axis=0)


def wait_bytes(sem, ref):
    pltpu.make_async_copy(ref, ref, sem).wait()


def kernel(
    nt, ntp, ny, tokens, mixw, pw, pmap, cot, projected, token_grad, proj_grad,
    xs, yt, xr, gs, ut, vt, onehot, cf, cx, pool, px, ps, pr, cs, cr, send, recv, ready,
):
    me = lax.axis_index("tok")
    mytp = lax.axis_index("tp")
    feats = tokens.shape[1]
    blocks = tokens.shape[0] // BLK
    groups = nt // blocks
    frows = feats // groups
    npool = cot.shape[0]
    equart = cot.shape[1]
    others = nt // NX
    mex, mehi = lax.rem(me, NX), lax.div(me, NX)

    barrier = pltpu.get_barrier_semaphore()
    plane = nt // ny
    myy, myp = lax.div(me, plane), lax.rem(me, plane)

    def greet(i, c):
        d = myy * plane + lax.rem(myp + i, plane)
        pl.semaphore_signal(barrier, inc=1, device_id={"tok": d}, device_id_type=MESH)
        return c

    def greet_line(i, c):
        d = lax.rem(myy + i, ny) * plane + myp
        pl.semaphore_signal(barrier, inc=1, device_id={"tok": d}, device_id_type=MESH)
        return c

    lax.fori_loop(1, plane, greet, 0)
    lax.fori_loop(1, ny, greet_line, 0)
    for i in range(1, ntp):
        pl.semaphore_signal(barrier, inc=1, device_id={"tp": lax.rem(mytp + i, ntp)}, device_id_type=MESH)

    def exchange(kind, src, dst):
        def one(i, c):
            d = lax.rem(me + i, nt)
            pltpu.make_async_remote_copy(
                src_ref=src.at[d], dst_ref=dst.at[me], send_sem=send.at[kind], recv_sem=recv.at[kind],
                device_id={"tok": d}, device_id_type=MESH,
            ).start()
            return c

        pltpu.make_async_copy(src.at[me], dst.at[me], recv.at[kind]).start()
        lax.fori_loop(1, nt, one, 0)

    def remote(src, dst, kind, **to):
        return pltpu.make_async_remote_copy(
            src_ref=src, dst_ref=dst, send_sem=send.at[kind], recv_sem=recv.at[kind],
            device_id=to, device_id_type=MESH,
        )

    def load_block(ref, j):
        parts = [ref[g * blocks + j] for g in range(groups)]
        return jnp.concatenate(parts, axis=0) if groups > 1 else parts[0]

    def store_block(ref, j, value):
        for g in range(groups):
            ref[g * blocks + j] = value[g * frows : (g + 1) * frows]

    def local_pairs(bit):
        return [(j, j | (1 << bit)) for j in range(blocks) if not j & (1 << bit)]

    cf[mytp] = cot[...].astype(jnp.float32).T.astype(jnp.bfloat16)

    w = section_matrix(mixw, 0)
    for lo, hi in local_pairs(0):
        out = mm(w, tokens[lo * BLK : (hi + 1) * BLK], NN).T.astype(jnp.bfloat16)
        store_block(xs, lo, out[:, :BLK])
        store_block(xs, hi, out[:, BLK:])
    for bit in (1, 2):
        w = section_matrix(mixw, bit)
        for lo, hi in local_pairs(bit):
            pair = jnp.concatenate([load_block(xs, lo), load_block(xs, hi)], axis=1)
            out = mm(pair, w, NT).astype(jnp.bfloat16)
            store_block(xs, lo, out[:, :BLK])
            store_block(xs, hi, out[:, BLK:])

    pl.semaphore_wait(barrier, plane - 1 + ny - 1 + ntp - 1)

    def announce(i, c):
        d = lax.rem(myy + i, ny) * plane + myp
        pl.semaphore_signal(ready.at[myy], inc=1, device_id={"tok": d}, device_id_type=MESH)
        return c

    lax.fori_loop(1, ny, announce, 0)
    mate, across_z, diagonal = mytp ^ 1, mytp ^ 2, mytp ^ 3
    remote(cf.at[mytp], cf.at[mytp], COTZ, tp=across_z).start()
    remote(cf.at[mytp], cf.at[mytp], COT, tp=mate).start()

    pltpu.make_async_copy(xs.at[me], yt.at[me], recv.at[F_IN]).start()
    for k in range(ny):
        step = (k + 1) // 2 if k % 2 else ny - k // 2
        y = lax.rem(myy + step, ny)
        if k > 0:
            pl.semaphore_wait(ready.at[y], 1)

        def to_plane(i, c, y=y):
            d = y * plane + lax.rem(myp + i, plane)
            remote(xs.at[d], yt.at[me], F_IN, tok=d).start()
            return c

        lax.fori_loop(1 if k == 0 else 0, plane, to_plane, 0)

    pid = lax.broadcasted_iota(jnp.int32, (npool, BLK), 0) + me * npool
    for j in range(blocks):
        hit = pid == jnp.broadcast_to(pmap[j : j + 1, :], (npool, BLK))
        onehot[:, j * BLK : (j + 1) * BLK] = jnp.where(hit, 1.0, 0.0).astype(jnp.bfloat16)
    ones = jnp.ones((8, blocks * BLK), jnp.bfloat16)
    counts_row = mm(ones, onehot[...], NT)[0:1]
    counts_col = jnp.sum(onehot[...].astype(jnp.float32), axis=1, keepdims=True)

    wait_bytes(recv.at[COTZ], cf.at[0])
    remote(cf.at[across_z], cf.at[across_z], COT, tp=mate).start()
    wait_bytes(recv.at[COT], cf.at[pl.ds(0, 2)])
    dp = mm(pw[:, 0:equart], cf[0], NN)
    for i in range(1, ntp):
        dp = dp + mm(pw[:, i * equart : (i + 1) * equart], cf[i], NN)
    dp = (dp / counts_row).astype(jnp.bfloat16)
    for j in range(blocks):
        store_block(gs, j, mm(dp, onehot[:, j * BLK : (j + 1) * BLK], NN).astype(jnp.bfloat16))
    exchange(B_IN, gs, ut)

    for i in range(NX):
        dx = lax.rem(mex + i, NX)
        if i == 0:
            pltpu.make_async_copy(cf.at[dx], cx.at[mex], recv.at[COTX]).start()
        else:
            pltpu.make_async_remote_copy(
                src_ref=cf.at[dx], dst_ref=cx.at[mex], send_sem=send.at[COTX], recv_sem=recv.at[COTX],
                device_id={"tok": mehi * NX + dx}, device_id_type=MESH,
            ).start()

    def across(ref, bit, s, dims):
        w = section_matrix(mixw, s)
        stride = 1 << bit
        half = nt // 2
        run = min(16, half)

        for c in range(half // run):
            if stride >= run:
                p = c * run
                lo = (p // stride) * (2 * stride) + p % stride
                a = ref[lo : lo + run].reshape(run * frows, BLK)
                b = ref[lo + stride : lo + stride + run].reshape(run * frows, BLK)
                out = mm(jnp.concatenate([a, b], axis=1), w, dims).astype(jnp.bfloat16)
                ref[lo : lo + run] = out[:, :BLK].reshape(run, frows, BLK)
                ref[lo + stride : lo + stride + run] = out[:, BLK:].reshape(run, frows, BLK)
            else:
                base = c * 2 * run
                v = ref[base : base + 2 * run].reshape(run // stride, 2, stride, frows, BLK)
                a = v[:, 0].reshape(run * frows, BLK)
                b = v[:, 1].reshape(run * frows, BLK)
                out = mm(jnp.concatenate([a, b], axis=1), w, dims).astype(jnp.bfloat16)
                a = out[:, :BLK].reshape(run // stride, 1, stride, frows, BLK)
                b = out[:, BLK:].reshape(run // stride, 1, stride, frows, BLK)
                ref[base : base + 2 * run] = jnp.concatenate([a, b], axis=1).reshape(2 * run, frows, BLK)

    bits = nt.bit_length() - 1
    wait_bytes(recv.at[F_IN], yt)
    for bit in range(bits):
        across(yt, bit, 3 + bit, NT)
    exchange(F_OUT, yt, xr)

    wait_bytes(recv.at[B_IN], ut)
    for bit in reversed(range(bits)):
        across(ut, bit, 3 + bit, NN)
    exchange(B_OUT, ut, vt)

    wait_bytes(recv.at[F_OUT], xr)
    total = mm(onehot[:, 0:BLK], load_block(xr, 0), NT)
    for j in range(1, blocks):
        total = total + mm(onehot[:, j * BLK : (j + 1) * BLK], load_block(xr, j), NT)
    pool[...] = (total / counts_col).astype(jnp.bfloat16)
    for i in range(NX):
        dx = lax.rem(mex + i, NX)
        if i == 0:
            pltpu.make_async_copy(pool, px.at[mex], recv.at[POOLX]).start()
        else:
            pltpu.make_async_remote_copy(
                src_ref=pool, dst_ref=px.at[mex], send_sem=send.at[POOLX], recv_sem=recv.at[POOLX],
                device_id={"tok": mehi * NX + dx}, device_id_type=MESH,
            ).start()
    for i in range(ntp):
        ps[i] = mm(pool[...], pw[:, i * equart : (i + 1) * equart], NN).astype(jnp.bfloat16)
    remote(ps.at[mate], pr.at[0], PROJ, tp=mate).start()
    remote(ps.at[diagonal], pr.at[1], PROJ, tp=mate).start()

    wait_bytes(recv.at[COTX], cx)
    wait_bytes(recv.at[POOLX], px)
    erows = equart // others
    parts = min(4, others)
    half = equart // parts
    for r in range(parts):
        part = mm(cx[0, r * half : (r + 1) * half], px[0], NN)
        for i in range(1, NX):
            part = part + mm(cx[i, r * half : (r + 1) * half], px[i], NN)
        n = others // parts
        cs[r * n : (r + 1) * n] = part.astype(jnp.bfloat16).reshape(n, erows, feats)

    wait_bytes(recv.at[PROJ], pr.at[pl.ds(0, 2)])
    far = ps[across_z].astype(jnp.float32) + pr[1].astype(jnp.float32)
    pr[2] = far.astype(jnp.bfloat16)
    remote(pr.at[2], pr.at[3], PROJZ, tp=across_z).start()

    def give(i, c):
        b = lax.rem(mehi + i, others)
        d = mex * others + b

        @pl.when(d == me)
        def _():
            pltpu.make_async_copy(cs.at[b], cr.at[mehi], recv.at[GRAD]).start()

        @pl.when(d != me)
        def _():
            pltpu.make_async_remote_copy(
                src_ref=cs.at[b], dst_ref=cr.at[mehi], send_sem=send.at[GRAD], recv_sem=recv.at[GRAD],
                device_id={"tok": d}, device_id_type=MESH,
            ).start()

        return c

    lax.fori_loop(0, others, give, 0)

    wait_bytes(recv.at[B_OUT], vt)
    for bit in (2, 1):
        w = section_matrix(mixw, bit)
        for lo, hi in local_pairs(bit):
            pair = jnp.concatenate([load_block(vt, lo), load_block(vt, hi)], axis=1)
            out = mm(pair, w, NN).astype(jnp.bfloat16)
            store_block(vt, lo, out[:, :BLK])
            store_block(vt, hi, out[:, BLK:])
    w = section_matrix(mixw, 0)
    for lo, hi in local_pairs(0):
        pair = jnp.concatenate([load_block(vt, lo), load_block(vt, hi)], axis=1)
        token_grad[lo * BLK : (hi + 1) * BLK] = mm(pair, w, NN).T.astype(jnp.bfloat16)

    wait_bytes(recv.at[PROJZ], pr.at[3])
    near = ps[mytp].astype(jnp.float32) + pr[0].astype(jnp.float32)
    projected[...] = (near + pr[3].astype(jnp.float32)).astype(jnp.bfloat16)

    wait_bytes(recv.at[GRAD], cr)
    proj_grad[...] = jnp.sum(cr[...].astype(jnp.float32), axis=0) * (1.0 / math.sqrt(npool * nt))

    for kind, ref in ((F_IN, yt), (B_IN, ut), (F_OUT, xr), (B_OUT, vt)):
        wait_bytes(send.at[kind], ref.at[pl.ds(0, nt - 1)])
    wait_bytes(send.at[COT], cf.at[pl.ds(0, 2)])
    wait_bytes(send.at[COTZ], cf.at[0])
    wait_bytes(send.at[PROJ], pr.at[pl.ds(0, 2)])
    wait_bytes(send.at[PROJZ], pr.at[0])
    wait_bytes(send.at[COTX], cx.at[pl.ds(0, NX - 1)])
    wait_bytes(send.at[POOLX], px.at[pl.ds(0, NX - 1)])
    mine = lax.div(me, others) == mex

    @pl.when(mine)
    def _():
        wait_bytes(send.at[GRAD], cr.at[pl.ds(0, others - 1)])

    @pl.when(jnp.logical_not(mine))
    def _():
        wait_bytes(send.at[GRAD], cr)


def shards(nt, ntp, ny, tokens, mixw, pw, pool_map, cot):
    rows, feats = tokens.shape
    blocks = rows // BLK
    frows = feats * blocks // nt
    npool, equart = cot.shape
    others = nt // NX
    erows = equart // others
    bf = jnp.bfloat16
    tiles = pltpu.VMEM((nt, frows, BLK), bf)
    vmem = pl.BlockSpec(memory_space=pltpu.VMEM)
    return pl.pallas_call(
        functools.partial(kernel, nt, ntp, ny),
        out_shape=(
            jax.ShapeDtypeStruct((npool, equart), bf),
            jax.ShapeDtypeStruct((rows, feats), bf),
            jax.ShapeDtypeStruct((erows, feats), jnp.float32),
        ),
        in_specs=[vmem] * 5,
        out_specs=(vmem,) * 3,
        scratch_shapes=[
            tiles, tiles, tiles, tiles, tiles, tiles,
            pltpu.VMEM((npool, rows), bf),
            pltpu.VMEM((ntp, equart, npool), bf),
            pltpu.VMEM((NX, equart, npool), bf),
            pltpu.VMEM((npool, feats), bf),
            pltpu.VMEM((NX, npool, feats), bf),
            pltpu.VMEM((ntp, npool, equart), bf),
            pltpu.VMEM((ntp, npool, equart), bf),
            pltpu.VMEM((others, erows, feats), bf),
            pltpu.VMEM((others, erows, feats), bf),
            pltpu.SemaphoreType.DMA((11,)),
            pltpu.SemaphoreType.DMA((11,)),
            pltpu.SemaphoreType.REGULAR((ny,)),
        ],
        compiler_params=pltpu.CompilerParams(collective_id=0, has_side_effects=True, vmem_limit_bytes=14 << 20),
    )(tokens, mixw, pw, pool_map.reshape(blocks, BLK), cot)


def solution(mesh):
    nt, ntp = mesh.shape["tok"], mesh.shape["tp"]
    return jax.shard_map(
        functools.partial(shards, nt, ntp, nt // 16),
        mesh=mesh,
        in_specs=(P("tok", "tp"), P(), P("tp", None), P("tok"), P("tok", "tp")),
        out_specs=(P("tok", "tp"), P("tok", "tp"), P("tok", "tp")),
        check_vma=False,
    )
```

```python
import functools
import math

import jax
import jax.numpy as jnp
from jax import lax
from jax.experimental import pallas as pl
from jax.experimental.pallas import tpu as pltpu
from jax.sharding import PartitionSpec as P

MESH = pl.DeviceIdType.MESH
BLK = 128
NX = 4
NN = (((1,), (0,)), ((), ()))
NT = (((1,), (1,)), ((), ()))
F_IN, F_OUT, B_IN, B_OUT, COT, COTX, POOLX, PROJ, GRAD, COTZ, PROJZ = range(11)


def mm(a, b, dims):
    return lax.dot_general(a, b, dims, preferred_element_type=jnp.float32)


def section_matrix(mixw, s):
    top = jnp.concatenate([mixw[s, 0, 0], mixw[s, 0, 1]], axis=1)
    low = jnp.concatenate([mixw[s, 1, 0], mixw[s, 1, 1]], axis=1)
    return jnp.concatenate([top, low], axis=0)


def wait_bytes(sem, ref):
    pltpu.make_async_copy(ref, ref, sem).wait()


def kernel(
    nt, ntp, ny, tokens_h, mixw_h, pw_h, pmap_h, cot_h, projected, token_grad, proj_grad,
    tokens, mixw, pw, pmap, cot, load, xs, yt, xr, gs, ut, vt, onehot, cf, cx, pool, px, ps, pr, cs, cr, send, recv, ready,
):
    me = lax.axis_index("tok")
    mytp = lax.axis_index("tp")
    rows, feats = tokens.shape
    blocks = rows // BLK
    groups = nt // blocks
    frows = feats // groups
    npool = cot.shape[0]
    equart = cot.shape[1]
    others = nt // NX
    erows = proj_grad.shape[0]
    mex, mehi = lax.rem(me, NX), lax.div(me, NX)

    loads = [
        pltpu.make_async_copy(cot_h, cot, load.at[0]),
        pltpu.make_async_copy(tokens_h, tokens, load.at[1]),
        pltpu.make_async_copy(mixw_h.at[0:3], mixw.at[0:3], load.at[2]),
        pltpu.make_async_copy(pmap_h, pmap, load.at[3]),
        pltpu.make_async_copy(pw_h, pw, load.at[4]),
        pltpu.make_async_copy(mixw_h.at[3:], mixw.at[3:], load.at[5]),
    ]
    for one in loads:
        one.start()

    barrier = pltpu.get_barrier_semaphore()
    plane = nt // ny
    myy, myp = lax.div(me, plane), lax.rem(me, plane)

    def greet(i, c):
        d = myy * plane + lax.rem(myp + i, plane)
        pl.semaphore_signal(barrier, inc=1, device_id={"tok": d}, device_id_type=MESH)
        return c

    def greet_line(i, c):
        d = lax.rem(myy + i, ny) * plane + myp
        pl.semaphore_signal(barrier, inc=1, device_id={"tok": d}, device_id_type=MESH)
        return c

    lax.fori_loop(1, plane, greet, 0)
    lax.fori_loop(1, ny, greet_line, 0)
    for i in range(1, ntp):
        pl.semaphore_signal(barrier, inc=1, device_id={"tp": lax.rem(mytp + i, ntp)}, device_id_type=MESH)

    def exchange(kind, src, dst, first=0, last=nt):
        def one(i, c):
            d = lax.rem(me + i, nt)
            pltpu.make_async_remote_copy(
                src_ref=src.at[d], dst_ref=dst.at[me], send_sem=send.at[kind], recv_sem=recv.at[kind],
                device_id={"tok": d}, device_id_type=MESH,
            ).start()
            return c

        if first == 0:
            pltpu.make_async_copy(src.at[me], dst.at[me], recv.at[kind]).start()
        lax.fori_loop(max(first, 1), last, one, 0)

    def remote(src, dst, kind, **to):
        return pltpu.make_async_remote_copy(
            src_ref=src, dst_ref=dst, send_sem=send.at[kind], recv_sem=recv.at[kind],
            device_id=to, device_id_type=MESH,
        )

    def load_block(ref, j):
        parts = [ref[g * blocks + j] for g in range(groups)]
        return jnp.concatenate(parts, axis=0) if groups > 1 else parts[0]

    def store_block(ref, j, value):
        for g in range(groups):
            ref[g * blocks + j] = value[g * frows : (g + 1) * frows]

    def local_pairs(bit):
        return [(j, j | (1 << bit)) for j in range(blocks) if not j & (1 << bit)]

    loads[0].wait()
    cf[mytp] = cot[...].astype(jnp.float32).T.astype(jnp.bfloat16).reshape(cf.shape[1:])

    loads[1].wait()
    loads[2].wait()
    w = section_matrix(mixw, 0)
    for lo, hi in local_pairs(0):
        out = mm(w, tokens[lo * BLK : (hi + 1) * BLK], NN).T.astype(jnp.bfloat16)
        store_block(xs, lo, out[:, :BLK])
        store_block(xs, hi, out[:, BLK:])
    for bit in (1, 2):
        w = section_matrix(mixw, bit)
        for lo, hi in local_pairs(bit):
            pair = jnp.concatenate([load_block(xs, lo), load_block(xs, hi)], axis=1)
            out = mm(pair, w, NT).astype(jnp.bfloat16)
            store_block(xs, lo, out[:, :BLK])
            store_block(xs, hi, out[:, BLK:])

    pl.semaphore_wait(barrier, plane - 1 + ny - 1 + ntp - 1)

    def announce(i, c):
        d = lax.rem(myy + i, ny) * plane + myp
        pl.semaphore_signal(ready.at[myy], inc=1, device_id={"tok": d}, device_id_type=MESH)
        return c

    lax.fori_loop(1, ny, announce, 0)
    mate, across_z, diagonal = mytp ^ 1, mytp ^ 2, mytp ^ 3
    remote(cf.at[mytp], cf.at[mytp], COTZ, tp=across_z).start()
    remote(cf.at[mytp], cf.at[mytp], COT, tp=mate).start()

    pltpu.make_async_copy(xs.at[me], yt.at[me], recv.at[F_IN]).start()
    for k in range(ny):
        step = (k + 1) // 2 if k % 2 else ny - k // 2
        y = lax.rem(myy + step, ny)
        if k > 0:
            pl.semaphore_wait(ready.at[y], 1)

        def to_plane(i, c, y=y):
            d = y * plane + lax.rem(myp + i, plane)
            remote(xs.at[d], yt.at[me], F_IN, tok=d).start()
            return c

        lax.fori_loop(1 if k == 0 else 0, plane, to_plane, 0)

    loads[3].wait()
    pid = lax.broadcasted_iota(jnp.int32, (npool, BLK), 0) + me * npool
    for j in range(blocks):
        hit = pid == jnp.broadcast_to(pmap[j : j + 1, :], (npool, BLK))
        onehot[:, j * BLK : (j + 1) * BLK] = jnp.where(hit, 1.0, 0.0).astype(jnp.bfloat16)
    ones = jnp.ones((8, blocks * BLK), jnp.bfloat16)
    counts_row = mm(ones, onehot[...], NT)[0:1]
    counts_col = jnp.sum(onehot[...].astype(jnp.float32), axis=1, keepdims=True)

    wait_bytes(recv.at[COTZ], cf.at[0])
    remote(cf.at[across_z], cf.at[across_z], COT, tp=mate).start()
    wait_bytes(recv.at[COT], cf.at[pl.ds(0, 2)])
    loads[4].wait()
    dp = mm(pw[:, 0:equart], cf[0].reshape(equart, npool), NN)
    for i in range(1, ntp):
        dp = dp + mm(pw[:, i * equart : (i + 1) * equart], cf[i].reshape(equart, npool), NN)
    dp = (dp / counts_row).astype(jnp.bfloat16)
    for j in range(blocks):
        store_block(gs, j, mm(dp, onehot[:, j * BLK : (j + 1) * BLK], NN).astype(jnp.bfloat16))
    exchange(B_IN, gs, ut)

    for i in range(NX):
        dx = lax.rem(mex + i, NX)
        if i == 0:
            pltpu.make_async_copy(cf.at[:, :, dx], cx.at[mex], recv.at[COTX]).start()
        else:
            pltpu.make_async_remote_copy(
                src_ref=cf.at[:, :, dx], dst_ref=cx.at[mex], send_sem=send.at[COTX], recv_sem=recv.at[COTX],
                device_id={"tok": mehi * NX + dx}, device_id_type=MESH,
            ).start()

    def across(ref, bit, s, dims):
        w = section_matrix(mixw, s)
        stride = 1 << bit
        half = nt // 2
        run = min(16, half)

        for c in range(half // run):
            if stride >= run:
                p = c * run
                lo = (p // stride) * (2 * stride) + p % stride
                a = ref[lo : lo + run].reshape(run * frows, BLK)
                b = ref[lo + stride : lo + stride + run].reshape(run * frows, BLK)
                out = mm(jnp.concatenate([a, b], axis=1), w, dims).astype(jnp.bfloat16)
                ref[lo : lo + run] = out[:, :BLK].reshape(run, frows, BLK)
                ref[lo + stride : lo + stride + run] = out[:, BLK:].reshape(run, frows, BLK)
            else:
                base = c * 2 * run
                v = ref[base : base + 2 * run].reshape(run // stride, 2, stride, frows, BLK)
                a = v[:, 0].reshape(run * frows, BLK)
                b = v[:, 1].reshape(run * frows, BLK)
                out = mm(jnp.concatenate([a, b], axis=1), w, dims).astype(jnp.bfloat16)
                a = out[:, :BLK].reshape(run // stride, 1, stride, frows, BLK)
                b = out[:, BLK:].reshape(run // stride, 1, stride, frows, BLK)
                ref[base : base + 2 * run] = jnp.concatenate([a, b], axis=1).reshape(2 * run, frows, BLK)

    bits = nt.bit_length() - 1
    loads[5].wait()
    wait_bytes(recv.at[F_IN], yt)
    for bit in range(bits):
        across(yt, bit, 3 + bit, NT)
    exchange(F_OUT, yt, xr)

    wait_bytes(recv.at[B_IN], ut)
    for bit in reversed(range(bits)):
        across(ut, bit, 3 + bit, NN)
    exchange(B_OUT, ut, vt, 0, nt // 2)

    wait_bytes(recv.at[F_OUT], xr)
    total = mm(onehot[:, 0:BLK], load_block(xr, 0), NT)
    for j in range(1, blocks):
        total = total + mm(onehot[:, j * BLK : (j + 1) * BLK], load_block(xr, j), NT)
    pool[...] = (total / counts_col).astype(jnp.bfloat16)
    for i in range(NX):
        dx = lax.rem(mex + i, NX)
        if i == 0:
            pltpu.make_async_copy(pool, px.at[mex], recv.at[POOLX]).start()
        else:
            pltpu.make_async_remote_copy(
                src_ref=pool, dst_ref=px.at[mex], send_sem=send.at[POOLX], recv_sem=recv.at[POOLX],
                device_id={"tok": mehi * NX + dx}, device_id_type=MESH,
            ).start()
    for i in range(ntp):
        ps[i] = mm(pool[...], pw[:, i * equart : (i + 1) * equart], NN).astype(jnp.bfloat16)
    remote(ps.at[mate], pr.at[0], PROJ, tp=mate).start()
    remote(ps.at[diagonal], pr.at[1], PROJ, tp=mate).start()
    exchange(B_OUT, ut, vt, nt // 2, nt)

    wait_bytes(recv.at[COTX], cx)
    wait_bytes(recv.at[POOLX], px)
    for q in range(ntp):
        n = others // ntp
        part = mm(cx[0, q].reshape(n * erows, npool), px[0], NN)
        for i in range(1, NX):
            part = part + mm(cx[i, q].reshape(n * erows, npool), px[i], NN)
        cs[q * n : (q + 1) * n] = part.astype(jnp.bfloat16).reshape(n, erows, feats)

    def give(i, c):
        b = lax.rem(mehi + i, others)
        remote(cs.at[b], cr.at[mehi], GRAD, tok=b * NX + mex).start()
        return c

    pltpu.make_async_copy(cs.at[mehi], cr.at[mehi], recv.at[GRAD]).start()
    lax.fori_loop(1, others, give, 0)

    wait_bytes(recv.at[PROJ], pr.at[pl.ds(0, 2)])
    far = ps[across_z].astype(jnp.float32) + pr[1].astype(jnp.float32)
    pr[2] = far.astype(jnp.bfloat16)
    remote(pr.at[2], pr.at[3], PROJZ, tp=across_z).start()

    wait_bytes(recv.at[B_OUT], vt)
    for bit in (2, 1):
        w = section_matrix(mixw, bit)
        for lo, hi in local_pairs(bit):
            pair = jnp.concatenate([load_block(vt, lo), load_block(vt, hi)], axis=1)
            out = mm(pair, w, NN).astype(jnp.bfloat16)
            store_block(vt, lo, out[:, :BLK])
            store_block(vt, hi, out[:, BLK:])
    w = section_matrix(mixw, 0)
    for lo, hi in local_pairs(0):
        pair = jnp.concatenate([load_block(vt, lo), load_block(vt, hi)], axis=1)
        token_grad[lo * BLK : (hi + 1) * BLK] = mm(pair, w, NN).T.astype(jnp.bfloat16)

    wait_bytes(recv.at[PROJZ], pr.at[3])
    near = ps[mytp].astype(jnp.float32) + pr[0].astype(jnp.float32)
    projected[...] = (near + pr[3].astype(jnp.float32)).astype(jnp.bfloat16)

    wait_bytes(recv.at[GRAD], cr)
    proj_grad[...] = jnp.sum(cr[...].astype(jnp.float32), axis=0) * (1.0 / math.sqrt(npool * nt))

    for kind, ref in ((F_IN, yt), (B_IN, ut), (F_OUT, xr), (B_OUT, vt)):
        wait_bytes(send.at[kind], ref.at[pl.ds(0, nt - 1)])
    wait_bytes(send.at[COT], cf.at[pl.ds(0, 2)])
    wait_bytes(send.at[COTZ], cf.at[0])
    wait_bytes(send.at[PROJ], pr.at[pl.ds(0, 2)])
    wait_bytes(send.at[PROJZ], pr.at[0])
    wait_bytes(send.at[COTX], cx.at[pl.ds(0, NX - 1)])
    wait_bytes(send.at[POOLX], px.at[pl.ds(0, NX - 1)])
    wait_bytes(send.at[GRAD], cr.at[pl.ds(0, others - 1)])


def shards(nt, ntp, ny, tokens, mixw, pw, pool_map, cot):
    rows, feats = tokens.shape
    blocks = rows // BLK
    frows = feats * blocks // nt
    npool, equart = cot.shape
    others = nt // NX
    erows = equart // others
    share = equart // (NX * erows)
    bf = jnp.bfloat16
    tiles = pltpu.VMEM((nt, frows, BLK), bf)
    vmem = pl.BlockSpec(memory_space=pltpu.VMEM)
    return pl.pallas_call(
        functools.partial(kernel, nt, ntp, ny),
        out_shape=(
            jax.ShapeDtypeStruct((npool, equart), bf),
            jax.ShapeDtypeStruct((rows, feats), bf),
            jax.ShapeDtypeStruct((erows, feats), jnp.float32),
        ),
        in_specs=[pl.BlockSpec(memory_space=pltpu.HBM)] * 5,
        out_specs=(vmem,) * 3,
        scratch_shapes=[
            pltpu.VMEM((rows, feats), bf),
            pltpu.VMEM(mixw.shape, bf),
            pltpu.VMEM(pw.shape, bf),
            pltpu.VMEM((blocks, BLK), jnp.int32),
            pltpu.VMEM((npool, equart), bf),
            pltpu.SemaphoreType.DMA((6,)),
            tiles, tiles, tiles, tiles, tiles, tiles,
            pltpu.VMEM((npool, rows), bf),
            pltpu.VMEM((ntp, share, NX, erows, npool), bf),
            pltpu.VMEM((NX, ntp, share, erows, npool), bf),
            pltpu.VMEM((npool, feats), bf),
            pltpu.VMEM((NX, npool, feats), bf),
            pltpu.VMEM((ntp, npool, equart), bf),
            pltpu.VMEM((ntp, npool, equart), bf),
            pltpu.VMEM((others, erows, feats), bf),
            pltpu.VMEM((others, erows, feats), bf),
            pltpu.SemaphoreType.DMA((11,)),
            pltpu.SemaphoreType.DMA((11,)),
            pltpu.SemaphoreType.REGULAR((ny,)),
        ],
        compiler_params=pltpu.CompilerParams(collective_id=0, has_side_effects=True, vmem_limit_bytes=18 << 20),
    )(tokens, mixw, pw, pool_map.reshape(blocks, BLK), cot)


def solution(mesh):
    nt, ntp = mesh.shape["tok"], mesh.shape["tp"]
    return jax.shard_map(
        functools.partial(shards, nt, ntp, nt // 16),
        mesh=mesh,
        in_specs=(P("tok", "tp"), P(), P("tp", None), P("tok"), P("tok", "tp")),
        out_specs=(P("tok", "tp"), P("tok", "tp"), P("tok", "tp")),
        check_vma=False,
    )
```

```python
import functools
import math

import jax
import jax.numpy as jnp
from jax import lax
from jax.experimental import pallas as pl
from jax.experimental.pallas import tpu as pltpu
from jax.sharding import PartitionSpec as P

MESH = pl.DeviceIdType.MESH
BLK = 128
NX = 4
NN = (((1,), (0,)), ((), ()))
NT = (((1,), (1,)), ((), ()))
F_IN, F_OUT, B_OUT, COT, COTX, POOLX, PROJ, GRAD, COTZ, PROJZ, DY, DZ, DX, MY, MZ, MX = range(16)


def mm(a, b, dims):
    return lax.dot_general(a, b, dims, preferred_element_type=jnp.float32)


def section_matrix(mixw, s):
    top = jnp.concatenate([mixw[s, 0, 0], mixw[s, 0, 1]], axis=1)
    low = jnp.concatenate([mixw[s, 1, 0], mixw[s, 1, 1]], axis=1)
    return jnp.concatenate([top, low], axis=0)


def wait_bytes(sem, ref):
    pltpu.make_async_copy(ref, ref, sem).wait()


def kernel(
    nt, ntp, ny, tokens_h, mixw_h, pw_h, pmap_h, cot_h, projected, token_grad, proj_grad,
    tokens, mixw, pw, pmap, cot, load, xs, yt, xr, ut, vt, d0, d1, d2, d3, m1, m2, m3, onehot, cf, cx, pool, px, ps, pr, cs, cr, send, recv, ready,
):
    me = lax.axis_index("tok")
    mytp = lax.axis_index("tp")
    rows, feats = tokens.shape
    blocks = rows // BLK
    groups = nt // blocks
    frows = feats // groups
    npool = cot.shape[0]
    equart = cot.shape[1]
    others = nt // NX
    erows = proj_grad.shape[0]
    mex, mehi = lax.rem(me, NX), lax.div(me, NX)
    nz = nt // (ny * NX)
    myz = lax.rem(mehi, nz)

    loads = [
        pltpu.make_async_copy(cot_h, cot, load.at[0]),
        pltpu.make_async_copy(tokens_h, tokens, load.at[1]),
        pltpu.make_async_copy(mixw_h.at[0:3], mixw.at[0:3], load.at[2]),
        pltpu.make_async_copy(pmap_h, pmap, load.at[3]),
        pltpu.make_async_copy(pw_h, pw, load.at[4]),
        pltpu.make_async_copy(mixw_h.at[3:], mixw.at[3:], load.at[5]),
    ]
    for one in loads:
        one.start()

    barrier = pltpu.get_barrier_semaphore()
    plane = nt // ny
    myy, myp = lax.div(me, plane), lax.rem(me, plane)

    def greet(i, c):
        d = myy * plane + lax.rem(myp + i, plane)
        pl.semaphore_signal(barrier, inc=1, device_id={"tok": d}, device_id_type=MESH)
        return c

    def greet_line(i, c):
        d = lax.rem(myy + i, ny) * plane + myp
        pl.semaphore_signal(barrier, inc=1, device_id={"tok": d}, device_id_type=MESH)
        return c

    lax.fori_loop(1, plane, greet, 0)
    lax.fori_loop(1, ny, greet_line, 0)
    for i in range(1, ntp):
        pl.semaphore_signal(barrier, inc=1, device_id={"tp": lax.rem(mytp + i, ntp)}, device_id_type=MESH)

    def exchange(kind, src, dst, first=0, last=nt):
        def one(i, c):
            d = lax.rem(me + i, nt)
            pltpu.make_async_remote_copy(
                src_ref=src.at[d], dst_ref=dst.at[me], send_sem=send.at[kind], recv_sem=recv.at[kind],
                device_id={"tok": d}, device_id_type=MESH,
            ).start()
            return c

        if first == 0:
            pltpu.make_async_copy(src.at[me], dst.at[me], recv.at[kind]).start()
        lax.fori_loop(max(first, 1), last, one, 0)

    def remote(src, dst, kind, **to):
        return pltpu.make_async_remote_copy(
            src_ref=src, dst_ref=dst, send_sem=send.at[kind], recv_sem=recv.at[kind],
            device_id=to, device_id_type=MESH,
        )

    def load_block(ref, j):
        parts = [ref[g * blocks + j] for g in range(groups)]
        return jnp.concatenate(parts, axis=0) if groups > 1 else parts[0]

    def store_block(ref, j, value):
        for g in range(groups):
            ref[g * blocks + j] = value[g * frows : (g + 1) * frows]

    def local_pairs(bit):
        return [(j, j | (1 << bit)) for j in range(blocks) if not j & (1 << bit)]

    loads[0].wait()
    cf[mytp] = cot[...].astype(jnp.float32).T.astype(jnp.bfloat16).reshape(cf.shape[1:])

    loads[1].wait()
    loads[2].wait()
    w = section_matrix(mixw, 0)
    for lo, hi in local_pairs(0):
        out = mm(w, tokens[lo * BLK : (hi + 1) * BLK], NN).T.astype(jnp.bfloat16)
        store_block(xs, lo, out[:, :BLK])
        store_block(xs, hi, out[:, BLK:])
    for bit in (1, 2):
        w = section_matrix(mixw, bit)
        for lo, hi in local_pairs(bit):
            pair = jnp.concatenate([load_block(xs, lo), load_block(xs, hi)], axis=1)
            out = mm(pair, w, NT).astype(jnp.bfloat16)
            store_block(xs, lo, out[:, :BLK])
            store_block(xs, hi, out[:, BLK:])

    pl.semaphore_wait(barrier, plane - 1 + ny - 1 + ntp - 1)

    def announce(i, c):
        d = lax.rem(myy + i, ny) * plane + myp
        pl.semaphore_signal(ready.at[myy], inc=1, device_id={"tok": d}, device_id_type=MESH)
        return c

    lax.fori_loop(1, ny, announce, 0)
    mate, across_z, diagonal = mytp ^ 1, mytp ^ 2, mytp ^ 3
    remote(cf.at[mytp], cf.at[mytp], COTZ, tp=across_z).start()
    remote(cf.at[mytp], cf.at[mytp], COT, tp=mate).start()

    pltpu.make_async_copy(xs.at[me], yt.at[me], recv.at[F_IN]).start()
    for k in range(ny):
        step = (k + 1) // 2 if k % 2 else ny - k // 2
        y = lax.rem(myy + step, ny)
        if k > 0:
            pl.semaphore_wait(ready.at[y], 1)

        def to_plane(i, c, y=y):
            d = y * plane + lax.rem(myp + i, plane)
            remote(xs.at[d], yt.at[me], F_IN, tok=d).start()
            return c

        lax.fori_loop(1 if k == 0 else 0, plane, to_plane, 0)

    loads[3].wait()
    pid = lax.broadcasted_iota(jnp.int32, (npool, BLK), 0) + me * npool
    for j in range(blocks):
        hit = pid == jnp.broadcast_to(pmap[j], (npool, BLK))
        onehot[:, j * BLK : (j + 1) * BLK] = jnp.where(hit, 1.0, 0.0).astype(jnp.bfloat16)
    ones = jnp.ones((8, blocks * BLK), jnp.bfloat16)
    counts_row = mm(ones, onehot[...], NT)[0:1]
    counts_col = jnp.sum(onehot[...].astype(jnp.float32), axis=1, keepdims=True)

    wait_bytes(recv.at[COTZ], cf.at[0])
    remote(cf.at[across_z], cf.at[across_z], COT, tp=mate).start()
    wait_bytes(recv.at[COT], cf.at[pl.ds(0, 2)])
    loads[4].wait()
    dp = mm(pw[:, 0:equart], cf[0].reshape(equart, npool), NN)
    for i in range(1, ntp):
        dp = dp + mm(pw[:, i * equart : (i + 1) * equart], cf[i].reshape(equart, npool), NN)
    dp = (dp / counts_row).astype(jnp.bfloat16)
    d0[...] = dp.reshape(groups, frows, npool)

    def along(size, mine, target, pairs):
        for src, dst, kind in pairs:
            pltpu.make_async_copy(src(mine), dst, recv.at[kind]).start()
        for i in range(1, size):
            to = lax.rem(mine + i, size)
            for src, dst, kind in pairs:
                remote(src(to), dst, kind, tok=target(to)).start()

    along(
        ny, myy, lambda y: y * plane + myp,
        [(lambda y: d0.at[pl.ds(2 * y, 2)], d1.at[myy], DY), (lambda y: pmap, m1.at[myy], MY)],
    )

    for i in range(NX):
        dx = lax.rem(mex + i, NX)
        if i == 0:
            pltpu.make_async_copy(cf.at[:, :, dx], cx.at[mex], recv.at[COTX]).start()
        else:
            pltpu.make_async_remote_copy(
                src_ref=cf.at[:, :, dx], dst_ref=cx.at[mex], send_sem=send.at[COTX], recv_sem=recv.at[COTX],
                device_id={"tok": mehi * NX + dx}, device_id_type=MESH,
            ).start()

    def across(ref, bit, s, dims):
        w = section_matrix(mixw, s)
        stride = 1 << bit
        half = nt // 2
        run = min(16, half)

        for c in range(half // run):
            if stride >= run:
                p = c * run
                lo = (p // stride) * (2 * stride) + p % stride
                a = ref[lo : lo + run].reshape(run * frows, BLK)
                b = ref[lo + stride : lo + stride + run].reshape(run * frows, BLK)
                out = mm(jnp.concatenate([a, b], axis=1), w, dims).astype(jnp.bfloat16)
                ref[lo : lo + run] = out[:, :BLK].reshape(run, frows, BLK)
                ref[lo + stride : lo + stride + run] = out[:, BLK:].reshape(run, frows, BLK)
            else:
                base = c * 2 * run
                v = ref[base : base + 2 * run].reshape(run // stride, 2, stride, frows, BLK)
                a = v[:, 0].reshape(run * frows, BLK)
                b = v[:, 1].reshape(run * frows, BLK)
                out = mm(jnp.concatenate([a, b], axis=1), w, dims).astype(jnp.bfloat16)
                a = out[:, :BLK].reshape(run // stride, 1, stride, frows, BLK)
                b = out[:, BLK:].reshape(run // stride, 1, stride, frows, BLK)
                ref[base : base + 2 * run] = jnp.concatenate([a, b], axis=1).reshape(2 * run, frows, BLK)

    bits = nt.bit_length() - 1
    wait_bytes(recv.at[DY], d1)
    wait_bytes(recv.at[MY], m1)
    along(
        nz, myz, lambda z: myy * plane + z * NX + mex,
        [
            (lambda z: d1.at[:, lax.div(z, 2)], d2.at[myz], DZ),
            (lambda z: m1.at[:, pl.ds(lax.rem(z, 2) * NX, NX)], m2.at[myz], MZ),
        ],
    )

    loads[5].wait()
    wait_bytes(recv.at[F_IN], yt)
    for bit in range(bits):
        across(yt, bit, 3 + bit, NT)

    wait_bytes(recv.at[DZ], d2)
    wait_bytes(recv.at[MZ], m2)
    along(
        NX, mex, lambda x: mehi * NX + x,
        [(lambda x: d2, d3.at[mex], DX), (lambda x: m2.at[:, :, x], m3.at[mex], MX)],
    )
    exchange(F_OUT, yt, xr)

    wait_bytes(recv.at[DX], d3)
    wait_bytes(recv.at[MX], m3)
    rank = lax.broadcasted_iota(jnp.int32, (npool, BLK), 0)
    for t in range(nt):
        at = (t % NX, t // NX % nz, t // NX // nz)
        hit = rank == jnp.broadcast_to(m3[at] - t * npool, (npool, BLK))
        ut[t] = mm(d3[at], jnp.where(hit, 1.0, 0.0).astype(jnp.bfloat16), NN).astype(jnp.bfloat16)
    for bit in reversed(range(bits)):
        across(ut, bit, 3 + bit, NN)
    exchange(B_OUT, ut, vt, 0, nt // 2)

    wait_bytes(recv.at[F_OUT], xr)
    total = mm(onehot[:, 0:BLK], load_block(xr, 0), NT)
    for j in range(1, blocks):
        total = total + mm(onehot[:, j * BLK : (j + 1) * BLK], load_block(xr, j), NT)
    pool[...] = (total / counts_col).astype(jnp.bfloat16)
    for i in range(NX):
        dx = lax.rem(mex + i, NX)
        if i == 0:
            pltpu.make_async_copy(pool, px.at[mex], recv.at[POOLX]).start()
        else:
            pltpu.make_async_remote_copy(
                src_ref=pool, dst_ref=px.at[mex], send_sem=send.at[POOLX], recv_sem=recv.at[POOLX],
                device_id={"tok": mehi * NX + dx}, device_id_type=MESH,
            ).start()
    for i in range(ntp):
        ps[i] = mm(pool[...], pw[:, i * equart : (i + 1) * equart], NN).astype(jnp.bfloat16)
    remote(ps.at[mate], pr.at[0], PROJ, tp=mate).start()
    remote(ps.at[diagonal], pr.at[1], PROJ, tp=mate).start()
    exchange(B_OUT, ut, vt, nt // 2, nt)

    wait_bytes(recv.at[COTX], cx)
    wait_bytes(recv.at[POOLX], px)
    for q in range(ntp):
        n = others // ntp
        part = mm(cx[0, q].reshape(n * erows, npool), px[0], NN)
        for i in range(1, NX):
            part = part + mm(cx[i, q].reshape(n * erows, npool), px[i], NN)
        cs[q * n : (q + 1) * n] = part.astype(jnp.bfloat16).reshape(n, erows, feats)

    def give(i, c):
        b = lax.rem(mehi + i, others)
        remote(cs.at[b], cr.at[mehi], GRAD, tok=b * NX + mex).start()
        return c

    pltpu.make_async_copy(cs.at[mehi], cr.at[mehi], recv.at[GRAD]).start()
    lax.fori_loop(1, others, give, 0)

    wait_bytes(recv.at[PROJ], pr.at[pl.ds(0, 2)])
    far = ps[across_z].astype(jnp.float32) + pr[1].astype(jnp.float32)
    pr[2] = far.astype(jnp.bfloat16)
    remote(pr.at[2], pr.at[3], PROJZ, tp=across_z).start()

    wait_bytes(recv.at[B_OUT], vt)
    for bit in (2, 1):
        w = section_matrix(mixw, bit)
        for lo, hi in local_pairs(bit):
            pair = jnp.concatenate([load_block(vt, lo), load_block(vt, hi)], axis=1)
            out = mm(pair, w, NN).astype(jnp.bfloat16)
            store_block(vt, lo, out[:, :BLK])
            store_block(vt, hi, out[:, BLK:])
    w = section_matrix(mixw, 0)
    for lo, hi in local_pairs(0):
        pair = jnp.concatenate([load_block(vt, lo), load_block(vt, hi)], axis=1)
        token_grad[lo * BLK : (hi + 1) * BLK] = mm(pair, w, NN).T.astype(jnp.bfloat16)

    wait_bytes(recv.at[PROJZ], pr.at[3])
    near = ps[mytp].astype(jnp.float32) + pr[0].astype(jnp.float32)
    projected[...] = (near + pr[3].astype(jnp.float32)).astype(jnp.bfloat16)

    wait_bytes(recv.at[GRAD], cr)
    proj_grad[...] = jnp.sum(cr[...].astype(jnp.float32), axis=0) * (1.0 / math.sqrt(npool * nt))

    for kind, ref in ((F_IN, yt), (F_OUT, xr), (B_OUT, vt)):
        wait_bytes(send.at[kind], ref.at[pl.ds(0, nt - 1)])
    for kind, ref in ((DY, d1), (DZ, d2), (DX, d3), (MY, m1), (MZ, m2), (MX, m3)):
        wait_bytes(send.at[kind], ref.at[pl.ds(0, ref.shape[0] - 1)])
    wait_bytes(send.at[COT], cf.at[pl.ds(0, 2)])
    wait_bytes(send.at[COTZ], cf.at[0])
    wait_bytes(send.at[PROJ], pr.at[pl.ds(0, 2)])
    wait_bytes(send.at[PROJZ], pr.at[0])
    wait_bytes(send.at[COTX], cx.at[pl.ds(0, NX - 1)])
    wait_bytes(send.at[POOLX], px.at[pl.ds(0, NX - 1)])
    wait_bytes(send.at[GRAD], cr.at[pl.ds(0, others - 1)])


def shards(nt, ntp, ny, tokens, mixw, pw, pool_map, cot):
    rows, feats = tokens.shape
    blocks = rows // BLK
    groups = nt // blocks
    frows = feats // groups
    nz = nt // (ny * NX)
    npool, equart = cot.shape
    others = nt // NX
    erows = equart // others
    share = equart // (NX * erows)
    bf = jnp.bfloat16
    tiles = pltpu.VMEM((nt, frows, BLK), bf)
    vmem = pl.BlockSpec(memory_space=pltpu.VMEM)
    return pl.pallas_call(
        functools.partial(kernel, nt, ntp, ny),
        out_shape=(
            jax.ShapeDtypeStruct((npool, equart), bf),
            jax.ShapeDtypeStruct((rows, feats), bf),
            jax.ShapeDtypeStruct((erows, feats), jnp.float32),
        ),
        in_specs=[pl.BlockSpec(memory_space=pltpu.HBM)] * 5,
        out_specs=(vmem,) * 3,
        scratch_shapes=[
            pltpu.VMEM((rows, feats), bf),
            pltpu.VMEM(mixw.shape, bf),
            pltpu.VMEM(pw.shape, bf),
            pltpu.VMEM((blocks, 1, BLK), jnp.int32),
            pltpu.VMEM((npool, equart), bf),
            pltpu.SemaphoreType.DMA((6,)),
            tiles, tiles, tiles, tiles, tiles,
            pltpu.VMEM((groups, frows, npool), bf),
            pltpu.VMEM((ny, 2, frows, npool), bf),
            pltpu.VMEM((nz, ny, frows, npool), bf),
            pltpu.VMEM((NX, nz, ny, frows, npool), bf),
            pltpu.VMEM((ny, blocks, 1, BLK), jnp.int32),
            pltpu.VMEM((nz, ny, NX, 1, BLK), jnp.int32),
            pltpu.VMEM((NX, nz, ny, 1, BLK), jnp.int32),
            pltpu.VMEM((npool, rows), bf),
            pltpu.VMEM((ntp, share, NX, erows, npool), bf),
            pltpu.VMEM((NX, ntp, share, erows, npool), bf),
            pltpu.VMEM((npool, feats), bf),
            pltpu.VMEM((NX, npool, feats), bf),
            pltpu.VMEM((ntp, npool, equart), bf),
            pltpu.VMEM((ntp, npool, equart), bf),
            pltpu.VMEM((others, erows, feats), bf),
            pltpu.VMEM((others, erows, feats), bf),
            pltpu.SemaphoreType.DMA((16,)),
            pltpu.SemaphoreType.DMA((16,)),
            pltpu.SemaphoreType.REGULAR((ny,)),
        ],
        compiler_params=pltpu.CompilerParams(collective_id=0, has_side_effects=True, vmem_limit_bytes=18 << 20),
    )(*[pltpu.with_memory_space_constraint(a, pltpu.HBM) for a in (tokens, mixw, pw, pool_map.reshape(blocks, 1, BLK), cot)])


def solution(mesh):
    nt, ntp = mesh.shape["tok"], mesh.shape["tp"]
    return jax.shard_map(
        functools.partial(shards, nt, ntp, nt // 16),
        mesh=mesh,
        in_specs=(P("tok", "tp"), P(), P("tp", None), P("tok"), P("tok", "tp")),
        out_specs=(P("tok", "tp"), P("tok", "tp"), P("tok", "tp")),
        check_vma=False,
    )
```

```python
import functools
import math

import jax
import jax.numpy as jnp
from jax import lax
from jax.experimental import pallas as pl
from jax.experimental.pallas import tpu as pltpu
from jax.sharding import PartitionSpec as P

MESH = pl.DeviceIdType.MESH
BLK = 128
NX = 4
NN = (((1,), (0,)), ((), ()))
NT = (((1,), (1,)), ((), ()))
F_IN, F_OUT, B_OUT, COT, COTX, POOLX, PROJ, GRAD, COTZ, PROJZ, DY, DZ, MY, MZ = range(14)
DX, MX = 14, 18


def mm(a, b, dims):
    return lax.dot_general(a, b, dims, preferred_element_type=jnp.float32)


def section_matrix(mixw, s):
    top = jnp.concatenate([mixw[s, 0, 0], mixw[s, 0, 1]], axis=1)
    low = jnp.concatenate([mixw[s, 1, 0], mixw[s, 1, 1]], axis=1)
    return jnp.concatenate([top, low], axis=0)


def wait_bytes(sem, ref):
    pltpu.make_async_copy(ref, ref, sem).wait()


def kernel(
    nt, ntp, ny, tokens_h, mixw_h, pw_h, pmap_h, cot_h, projected, token_grad, proj_grad,
    tokens, mixw, pw, pmap, cot, load, xs, yt, xr, ut, vt, d0, d1, d2, d3, m1, m2, m3, onehot, cf, cx, pool, px, ps, pr, cs, cr, send, recv, ready,
):
    me = lax.axis_index("tok")
    mytp = lax.axis_index("tp")
    rows, feats = tokens.shape
    blocks = rows // BLK
    groups = nt // blocks
    frows = feats // groups
    npool = cot.shape[0]
    equart = cot.shape[1]
    others = nt // NX
    erows = proj_grad.shape[0]
    mex, mehi = lax.rem(me, NX), lax.div(me, NX)
    nz = nt // (ny * NX)
    myz = lax.rem(mehi, nz)

    loads = [
        pltpu.make_async_copy(cot_h, cot, load.at[0]),
        pltpu.make_async_copy(tokens_h, tokens, load.at[1]),
        pltpu.make_async_copy(mixw_h.at[0:3], mixw.at[0:3], load.at[2]),
        pltpu.make_async_copy(pmap_h, pmap, load.at[3]),
        pltpu.make_async_copy(pw_h, pw, load.at[4]),
        pltpu.make_async_copy(mixw_h.at[3:], mixw.at[3:], load.at[5]),
    ]
    for one in loads:
        one.start()

    barrier = pltpu.get_barrier_semaphore()
    plane = nt // ny
    myy, myp = lax.div(me, plane), lax.rem(me, plane)

    def greet(i, c):
        d = myy * plane + lax.rem(myp + i, plane)
        pl.semaphore_signal(barrier, inc=1, device_id={"tok": d}, device_id_type=MESH)
        return c

    def greet_line(i, c):
        d = lax.rem(myy + i, ny) * plane + myp
        pl.semaphore_signal(barrier, inc=1, device_id={"tok": d}, device_id_type=MESH)
        return c

    lax.fori_loop(1, plane, greet, 0)
    lax.fori_loop(1, ny, greet_line, 0)
    for i in range(1, ntp):
        pl.semaphore_signal(barrier, inc=1, device_id={"tp": lax.rem(mytp + i, ntp)}, device_id_type=MESH)

    def exchange(kind, src, dst, first=0, last=nt):
        def one(i, c):
            d = lax.rem(me + i, nt)
            pltpu.make_async_remote_copy(
                src_ref=src.at[d], dst_ref=dst.at[me], send_sem=send.at[kind], recv_sem=recv.at[kind],
                device_id={"tok": d}, device_id_type=MESH,
            ).start()
            return c

        if first == 0:
            pltpu.make_async_copy(src.at[me], dst.at[me], recv.at[kind]).start()
        lax.fori_loop(max(first, 1), last, one, 0)

    def remote(src, dst, kind, **to):
        return pltpu.make_async_remote_copy(
            src_ref=src, dst_ref=dst, send_sem=send.at[kind], recv_sem=recv.at[kind],
            device_id=to, device_id_type=MESH,
        )

    def load_block(ref, j):
        parts = [ref[g * blocks + j] for g in range(groups)]
        return jnp.concatenate(parts, axis=0) if groups > 1 else parts[0]

    def store_block(ref, j, value):
        for g in range(groups):
            ref[g * blocks + j] = value[g * frows : (g + 1) * frows]

    def local_pairs(bit):
        return [(j, j | (1 << bit)) for j in range(blocks) if not j & (1 << bit)]

    loads[0].wait()
    cf[mytp] = cot[...].astype(jnp.float32).T.astype(jnp.bfloat16).reshape(cf.shape[1:])

    loads[1].wait()
    loads[2].wait()
    w = section_matrix(mixw, 0)
    for lo, hi in local_pairs(0):
        out = mm(w, tokens[lo * BLK : (hi + 1) * BLK], NN).T.astype(jnp.bfloat16)
        store_block(xs, lo, out[:, :BLK])
        store_block(xs, hi, out[:, BLK:])
    for bit in (1, 2):
        w = section_matrix(mixw, bit)
        for lo, hi in local_pairs(bit):
            pair = jnp.concatenate([load_block(xs, lo), load_block(xs, hi)], axis=1)
            out = mm(pair, w, NT).astype(jnp.bfloat16)
            store_block(xs, lo, out[:, :BLK])
            store_block(xs, hi, out[:, BLK:])

    pl.semaphore_wait(barrier, plane - 1 + ny - 1 + ntp - 1)

    def announce(i, c):
        d = lax.rem(myy + i, ny) * plane + myp
        pl.semaphore_signal(ready.at[myy], inc=1, device_id={"tok": d}, device_id_type=MESH)
        return c

    lax.fori_loop(1, ny, announce, 0)
    mate, across_z, diagonal = mytp ^ 1, mytp ^ 2, mytp ^ 3
    remote(cf.at[mytp], cf.at[mytp], COTZ, tp=across_z).start()
    remote(cf.at[mytp], cf.at[mytp], COT, tp=mate).start()

    pltpu.make_async_copy(xs.at[me], yt.at[me], recv.at[F_IN]).start()
    order = [0] + sorted(range(1, ny), key=lambda step: -min(step, ny - step))

    def send_planes(steps):
        for step in steps:
            y = lax.rem(myy + step, ny)
            if step > 0:
                pl.semaphore_wait(ready.at[y], 1)

            def to_plane(i, c, y=y):
                d = y * plane + lax.rem(myp + i, plane)
                remote(xs.at[d], yt.at[me], F_IN, tok=d).start()
                return c

            lax.fori_loop(0 if step > 0 else 1, plane, to_plane, 0)

    send_planes(order[: ny // 2])

    loads[3].wait()
    pid = lax.broadcasted_iota(jnp.int32, (npool, BLK), 0) + me * npool
    for j in range(blocks):
        hit = pid == jnp.broadcast_to(pmap[j], (npool, BLK))
        onehot[:, j * BLK : (j + 1) * BLK] = jnp.where(hit, 1.0, 0.0).astype(jnp.bfloat16)
    ones = jnp.ones((8, blocks * BLK), jnp.bfloat16)
    counts_row = mm(ones, onehot[...], NT)[0:1]
    counts_col = jnp.sum(onehot[...].astype(jnp.float32), axis=1, keepdims=True)

    wait_bytes(recv.at[COTZ], cf.at[0])
    remote(cf.at[across_z], cf.at[across_z], COT, tp=mate).start()
    wait_bytes(recv.at[COT], cf.at[pl.ds(0, 2)])
    loads[4].wait()
    dp = mm(pw[:, 0:equart], cf[0].reshape(equart, npool), NN)
    for i in range(1, ntp):
        dp = dp + mm(pw[:, i * equart : (i + 1) * equart], cf[i].reshape(equart, npool), NN)
    dp = (dp / counts_row).astype(jnp.bfloat16)
    d0[...] = dp.reshape(groups, frows, npool)

    def along(size, mine, target, pairs):
        for src, dst, kind in pairs:
            pltpu.make_async_copy(src(mine), dst, recv.at[kind]).start()
        for i in range(1, size):
            to = lax.rem(mine + i, size)
            for src, dst, kind in pairs:
                remote(src(to), dst, kind, tok=target(to)).start()

    along(
        ny, myy, lambda y: y * plane + myp,
        [(lambda y: d0.at[pl.ds(2 * y, 2)], d1.at[myy], DY), (lambda y: pmap, m1.at[myy], MY)],
    )

    send_planes(order[ny // 2 :])

    def across(ref, bit, s, dims):
        w = section_matrix(mixw, s)
        stride = 1 << bit
        half = nt // 2
        run = min(16, half)

        for c in range(half // run):
            if stride >= run:
                p = c * run
                lo = (p // stride) * (2 * stride) + p % stride
                a = ref[lo : lo + run].reshape(run * frows, BLK)
                b = ref[lo + stride : lo + stride + run].reshape(run * frows, BLK)
                out = mm(jnp.concatenate([a, b], axis=1), w, dims).astype(jnp.bfloat16)
                ref[lo : lo + run] = out[:, :BLK].reshape(run, frows, BLK)
                ref[lo + stride : lo + stride + run] = out[:, BLK:].reshape(run, frows, BLK)
            else:
                base = c * 2 * run
                v = ref[base : base + 2 * run].reshape(run // stride, 2, stride, frows, BLK)
                a = v[:, 0].reshape(run * frows, BLK)
                b = v[:, 1].reshape(run * frows, BLK)
                out = mm(jnp.concatenate([a, b], axis=1), w, dims).astype(jnp.bfloat16)
                a = out[:, :BLK].reshape(run // stride, 1, stride, frows, BLK)
                b = out[:, BLK:].reshape(run // stride, 1, stride, frows, BLK)
                ref[base : base + 2 * run] = jnp.concatenate([a, b], axis=1).reshape(2 * run, frows, BLK)

    bits = nt.bit_length() - 1
    wait_bytes(recv.at[DY], d1)
    wait_bytes(recv.at[MY], m1)
    along(
        nz, myz, lambda z: myy * plane + z * NX + mex,
        [
            (lambda z: d1.at[:, lax.div(z, 2)], d2.at[myz], DZ),
            (lambda z: m1.at[:, pl.ds(lax.rem(z, 2) * NX, NX)], m2.at[myz], MZ),
        ],
    )

    loads[5].wait()
    wait_bytes(recv.at[F_IN], yt)
    for bit in range(bits):
        across(yt, bit, 3 + bit, NT)

    wait_bytes(recv.at[DZ], d2)
    wait_bytes(recv.at[MZ], m2)
    for i in range(1, NX):
        x = lax.rem(mex + i, NX)
        remote(d2, d3.at[mex], DX + i, tok=mehi * NX + x).start()
        remote(m2.at[:, :, x], m3.at[mex], MX + i, tok=mehi * NX + x).start()
    exchange(F_OUT, yt, xr)

    for i in range(NX):
        dx = lax.rem(mex + i, NX)
        if i == 0:
            pltpu.make_async_copy(cf.at[:, :, dx], cx.at[mex], recv.at[COTX]).start()
        else:
            pltpu.make_async_remote_copy(
                src_ref=cf.at[:, :, dx], dst_ref=cx.at[mex], send_sem=send.at[COTX], recv_sem=recv.at[COTX],
                device_id={"tok": mehi * NX + dx}, device_id_type=MESH,
            ).start()

    rank = lax.broadcasted_iota(jnp.int32, (npool, BLK), 0)
    for i in range(NX):
        x = lax.rem(mex - i + NX, NX)
        if i > 0:
            wait_bytes(recv.at[DX + i], d2)
            wait_bytes(recv.at[MX + i], m3.at[0])
        for z in range(nz):
            for y in range(ny):
                t = (y * nz + z) * NX + x
                row = (m2[z, y, mex] if i == 0 else m3[x, z, y]) - t * npool
                hit = rank == jnp.broadcast_to(row, (npool, BLK))
                rows_in = d2[z, y] if i == 0 else d3[x, z, y]
                ut[t] = mm(rows_in, jnp.where(hit, 1.0, 0.0).astype(jnp.bfloat16), NN).astype(jnp.bfloat16)
    for bit in reversed(range(bits)):
        across(ut, bit, 3 + bit, NN)
    exchange(B_OUT, ut, vt, 0, nt // 2)

    wait_bytes(recv.at[F_OUT], xr)
    total = mm(onehot[:, 0:BLK], load_block(xr, 0), NT)
    for j in range(1, blocks):
        total = total + mm(onehot[:, j * BLK : (j + 1) * BLK], load_block(xr, j), NT)
    pool[...] = (total / counts_col).astype(jnp.bfloat16)
    for i in range(NX):
        dx = lax.rem(mex + i, NX)
        if i == 0:
            pltpu.make_async_copy(pool, px.at[mex], recv.at[POOLX]).start()
        else:
            pltpu.make_async_remote_copy(
                src_ref=pool, dst_ref=px.at[mex], send_sem=send.at[POOLX], recv_sem=recv.at[POOLX],
                device_id={"tok": mehi * NX + dx}, device_id_type=MESH,
            ).start()
    for i in range(ntp):
        ps[i] = mm(pool[...], pw[:, i * equart : (i + 1) * equart], NN).astype(jnp.bfloat16)
    remote(ps.at[mate], pr.at[0], PROJ, tp=mate).start()
    remote(ps.at[diagonal], pr.at[1], PROJ, tp=mate).start()
    exchange(B_OUT, ut, vt, nt // 2, nt)

    wait_bytes(recv.at[COTX], cx)
    wait_bytes(recv.at[POOLX], px)
    for q in range(ntp):
        n = others // ntp
        part = mm(cx[0, q].reshape(n * erows, npool), px[0], NN)
        for i in range(1, NX):
            part = part + mm(cx[i, q].reshape(n * erows, npool), px[i], NN)
        cs[q * n : (q + 1) * n] = part.astype(jnp.bfloat16).reshape(n, erows, feats)

    def give(i, c):
        b = lax.rem(mehi + i, others)
        remote(cs.at[b], cr.at[mehi], GRAD, tok=b * NX + mex).start()
        return c

    pltpu.make_async_copy(cs.at[mehi], cr.at[mehi], recv.at[GRAD]).start()
    lax.fori_loop(1, others, give, 0)

    wait_bytes(recv.at[PROJ], pr.at[pl.ds(0, 2)])
    far = ps[across_z].astype(jnp.float32) + pr[1].astype(jnp.float32)
    pr[2] = far.astype(jnp.bfloat16)
    remote(pr.at[2], pr.at[3], PROJZ, tp=across_z).start()

    wait_bytes(recv.at[B_OUT], vt)
    for bit in (2, 1):
        w = section_matrix(mixw, bit)
        for lo, hi in local_pairs(bit):
            pair = jnp.concatenate([load_block(vt, lo), load_block(vt, hi)], axis=1)
            out = mm(pair, w, NN).astype(jnp.bfloat16)
            store_block(vt, lo, out[:, :BLK])
            store_block(vt, hi, out[:, BLK:])
    w = section_matrix(mixw, 0)
    for lo, hi in local_pairs(0):
        pair = jnp.concatenate([load_block(vt, lo), load_block(vt, hi)], axis=1)
        token_grad[lo * BLK : (hi + 1) * BLK] = mm(pair, w, NN).T.astype(jnp.bfloat16)

    wait_bytes(recv.at[PROJZ], pr.at[3])
    near = ps[mytp].astype(jnp.float32) + pr[0].astype(jnp.float32)
    projected[...] = (near + pr[3].astype(jnp.float32)).astype(jnp.bfloat16)

    wait_bytes(recv.at[GRAD], cr)
    proj_grad[...] = jnp.sum(cr[...].astype(jnp.float32), axis=0) * (1.0 / math.sqrt(npool * nt))

    for kind, ref in ((F_IN, yt), (F_OUT, xr), (B_OUT, vt)):
        wait_bytes(send.at[kind], ref.at[pl.ds(0, nt - 1)])
    for i in range(1, NX):
        wait_bytes(send.at[DX + i], d2)
        wait_bytes(send.at[MX + i], m3.at[0])
    for kind, ref in ((DY, d1), (DZ, d2), (MY, m1), (MZ, m2)):
        wait_bytes(send.at[kind], ref.at[pl.ds(0, ref.shape[0] - 1)])
    wait_bytes(send.at[COT], cf.at[pl.ds(0, 2)])
    wait_bytes(send.at[COTZ], cf.at[0])
    wait_bytes(send.at[PROJ], pr.at[pl.ds(0, 2)])
    wait_bytes(send.at[PROJZ], pr.at[0])
    wait_bytes(send.at[COTX], cx.at[pl.ds(0, NX - 1)])
    wait_bytes(send.at[POOLX], px.at[pl.ds(0, NX - 1)])
    wait_bytes(send.at[GRAD], cr.at[pl.ds(0, others - 1)])


def shards(nt, ntp, ny, tokens, mixw, pw, pool_map, cot):
    rows, feats = tokens.shape
    blocks = rows // BLK
    groups = nt // blocks
    frows = feats // groups
    nz = nt // (ny * NX)
    npool, equart = cot.shape
    others = nt // NX
    erows = equart // others
    share = equart // (NX * erows)
    bf = jnp.bfloat16
    tiles = pltpu.VMEM((nt, frows, BLK), bf)
    vmem = pl.BlockSpec(memory_space=pltpu.VMEM)
    return pl.pallas_call(
        functools.partial(kernel, nt, ntp, ny),
        out_shape=(
            jax.ShapeDtypeStruct((npool, equart), bf),
            jax.ShapeDtypeStruct((rows, feats), bf),
            jax.ShapeDtypeStruct((erows, feats), jnp.float32),
        ),
        in_specs=[pl.BlockSpec(memory_space=pltpu.HBM)] * 5,
        out_specs=(vmem,) * 3,
        scratch_shapes=[
            pltpu.VMEM((rows, feats), bf),
            pltpu.VMEM(mixw.shape, bf),
            pltpu.VMEM(pw.shape, bf),
            pltpu.VMEM((blocks, 1, BLK), jnp.int32),
            pltpu.VMEM((npool, equart), bf),
            pltpu.SemaphoreType.DMA((6,)),
            tiles, tiles, tiles, tiles, tiles,
            pltpu.VMEM((groups, frows, npool), bf),
            pltpu.VMEM((ny, 2, frows, npool), bf),
            pltpu.VMEM((nz, ny, frows, npool), bf),
            pltpu.VMEM((NX, nz, ny, frows, npool), bf),
            pltpu.VMEM((ny, blocks, 1, BLK), jnp.int32),
            pltpu.VMEM((nz, ny, NX, 1, BLK), jnp.int32),
            pltpu.VMEM((NX, nz, ny, 1, BLK), jnp.int32),
            pltpu.VMEM((npool, rows), bf),
            pltpu.VMEM((ntp, share, NX, erows, npool), bf),
            pltpu.VMEM((NX, ntp, share, erows, npool), bf),
            pltpu.VMEM((npool, feats), bf),
            pltpu.VMEM((NX, npool, feats), bf),
            pltpu.VMEM((ntp, npool, equart), bf),
            pltpu.VMEM((ntp, npool, equart), bf),
            pltpu.VMEM((others, erows, feats), bf),
            pltpu.VMEM((others, erows, feats), bf),
            pltpu.SemaphoreType.DMA((22,)),
            pltpu.SemaphoreType.DMA((22,)),
            pltpu.SemaphoreType.REGULAR((ny,)),
        ],
        compiler_params=pltpu.CompilerParams(collective_id=0, has_side_effects=True, vmem_limit_bytes=18 << 20),
    )(*[pltpu.with_memory_space_constraint(a, pltpu.HBM) for a in (tokens, mixw, pw, pool_map.reshape(blocks, 1, BLK), cot)])


def solution(mesh):
    nt, ntp = mesh.shape["tok"], mesh.shape["tp"]
    return jax.shard_map(
        functools.partial(shards, nt, ntp, nt // 16),
        mesh=mesh,
        in_specs=(P("tok", "tp"), P(), P("tp", None), P("tok"), P("tok", "tp")),
        out_specs=(P("tok", "tp"), P("tok", "tp"), P("tok", "tp")),
        check_vma=False,
    )
```

```python
import functools
import math

import jax
import jax.numpy as jnp
from jax import lax
from jax.experimental import pallas as pl
from jax.experimental.pallas import tpu as pltpu
from jax.sharding import PartitionSpec as P

MESH = pl.DeviceIdType.MESH
BLK = 128
NX = 4
NN = (((1,), (0,)), ((), ()))
NT = (((1,), (1,)), ((), ()))
F_IN, F_OUT, B_OUT, COT, COTX, POOLX, PROJ, GRAD, COTZ, PROJZ, DY, DZ, MY, MZ = range(14)
DX, MX = 14, 18


def mm(a, b, dims):
    return lax.dot_general(a, b, dims, preferred_element_type=jnp.float32)


def section_matrix(mixw, s):
    top = jnp.concatenate([mixw[s, 0, 0], mixw[s, 0, 1]], axis=1)
    low = jnp.concatenate([mixw[s, 1, 0], mixw[s, 1, 1]], axis=1)
    return jnp.concatenate([top, low], axis=0)


def wait_bytes(sem, ref):
    pltpu.make_async_copy(ref, ref, sem).wait()


def kernel(
    nt, ntp, ny, tokens_h, mixw_h, pw_h, pmap_h, cot_h, projected, token_grad, proj_grad,
    tokens, mixw, pw, pmap, cot, load, xs, yt, xr, ut, vt, d0, d1, d2, d3, m1, m2, m3, onehot, cf, cx, pool, px, ps, pr, cs, cr, send, recv, ready,
):
    me = lax.axis_index("tok")
    mytp = lax.axis_index("tp")
    rows, feats = tokens.shape
    blocks = rows // BLK
    groups = nt // blocks
    frows = feats // groups
    npool = cot.shape[0]
    equart = cot.shape[1]
    others = nt // NX
    erows = proj_grad.shape[0]
    mex, mehi = lax.rem(me, NX), lax.div(me, NX)
    nz = nt // (ny * NX)
    myz = lax.rem(mehi, nz)

    loads = [
        pltpu.make_async_copy(cot_h, cot, load.at[0]),
        pltpu.make_async_copy(tokens_h, tokens, load.at[1]),
        pltpu.make_async_copy(mixw_h.at[0:3], mixw.at[0:3], load.at[2]),
        pltpu.make_async_copy(pmap_h, pmap, load.at[3]),
        pltpu.make_async_copy(pw_h, pw, load.at[4]),
        pltpu.make_async_copy(mixw_h.at[3:], mixw.at[3:], load.at[5]),
    ]
    for one in loads:
        one.start()

    barrier = pltpu.get_barrier_semaphore()
    plane = nt // ny
    myy, myp = lax.div(me, plane), lax.rem(me, plane)

    def greet(i, c):
        d = myy * plane + lax.rem(myp + i, plane)
        pl.semaphore_signal(barrier, inc=1, device_id={"tok": d}, device_id_type=MESH)
        return c

    def greet_line(i, c):
        d = lax.rem(myy + i, ny) * plane + myp
        pl.semaphore_signal(barrier, inc=1, device_id={"tok": d}, device_id_type=MESH)
        return c

    lax.fori_loop(1, plane, greet, 0)
    lax.fori_loop(1, ny, greet_line, 0)
    for i in range(1, ntp):
        pl.semaphore_signal(barrier, inc=1, device_id={"tp": lax.rem(mytp + i, ntp)}, device_id_type=MESH)

    def exchange(kind, src, dst, first=0, last=nt):
        def one(i, c):
            d = lax.rem(me + i, nt)
            pltpu.make_async_remote_copy(
                src_ref=src.at[d], dst_ref=dst.at[me], send_sem=send.at[kind], recv_sem=recv.at[kind],
                device_id={"tok": d}, device_id_type=MESH,
            ).start()
            return c

        if first == 0:
            pltpu.make_async_copy(src.at[me], dst.at[me], recv.at[kind]).start()
        lax.fori_loop(max(first, 1), last, one, 0)

    def remote(src, dst, kind, **to):
        return pltpu.make_async_remote_copy(
            src_ref=src, dst_ref=dst, send_sem=send.at[kind], recv_sem=recv.at[kind],
            device_id=to, device_id_type=MESH,
        )

    def load_block(ref, j):
        parts = [ref[g * blocks + j] for g in range(groups)]
        return jnp.concatenate(parts, axis=0) if groups > 1 else parts[0]

    def store_block(ref, j, value):
        for g in range(groups):
            ref[g * blocks + j] = value[g * frows : (g + 1) * frows]

    def local_pairs(bit):
        return [(j, j | (1 << bit)) for j in range(blocks) if not j & (1 << bit)]

    loads[0].wait()
    cf[mytp] = cot[...].astype(jnp.float32).T.astype(jnp.bfloat16).reshape(cf.shape[1:])

    loads[1].wait()
    loads[2].wait()
    w = section_matrix(mixw, 0)
    for lo, hi in local_pairs(0):
        out = mm(w, tokens[lo * BLK : (hi + 1) * BLK], NN).T.astype(jnp.bfloat16)
        store_block(xs, lo, out[:, :BLK])
        store_block(xs, hi, out[:, BLK:])
    for bit in (1, 2):
        w = section_matrix(mixw, bit)
        for lo, hi in local_pairs(bit):
            pair = jnp.concatenate([load_block(xs, lo), load_block(xs, hi)], axis=1)
            out = mm(pair, w, NT).astype(jnp.bfloat16)
            store_block(xs, lo, out[:, :BLK])
            store_block(xs, hi, out[:, BLK:])

    pl.semaphore_wait(barrier, plane - 1 + ny - 1 + ntp - 1)

    def announce(i, c):
        d = lax.rem(myy + i, ny) * plane + myp
        pl.semaphore_signal(ready.at[myy], inc=1, device_id={"tok": d}, device_id_type=MESH)
        return c

    lax.fori_loop(1, ny, announce, 0)
    mate, across_z, diagonal = mytp ^ 1, mytp ^ 2, mytp ^ 3
    remote(cf.at[mytp], cf.at[mytp], COTZ, tp=across_z).start()
    remote(cf.at[mytp], cf.at[mytp], COT, tp=mate).start()

    pltpu.make_async_copy(xs.at[me], yt.at[me], recv.at[F_IN]).start()
    order = [0] + sorted(range(1, ny), key=lambda step: -min(step, ny - step))

    def send_planes(steps):
        for step in steps:
            y = lax.rem(myy + step, ny)
            if step > 0:
                pl.semaphore_wait(ready.at[y], 1)

            def to_plane(i, c, y=y):
                d = y * plane + lax.rem(myp + i, plane)
                remote(xs.at[d], yt.at[me], F_IN, tok=d).start()
                return c

            lax.fori_loop(0 if step > 0 else 1, plane, to_plane, 0)

    send_planes(order[: ny // 2])

    loads[3].wait()
    pid = lax.broadcasted_iota(jnp.int32, (npool, BLK), 0) + me * npool
    for j in range(blocks):
        hit = pid == jnp.broadcast_to(pmap[j], (npool, BLK))
        onehot[:, j * BLK : (j + 1) * BLK] = jnp.where(hit, 1.0, 0.0).astype(jnp.bfloat16)
    ones = jnp.ones((8, blocks * BLK), jnp.bfloat16)
    counts_row = mm(ones, onehot[...], NT)[0:1]
    counts_col = jnp.sum(onehot[...].astype(jnp.float32), axis=1, keepdims=True)

    wait_bytes(recv.at[COTZ], cf.at[0])
    remote(cf.at[across_z], cf.at[across_z], COT, tp=mate).start()
    wait_bytes(recv.at[COT], cf.at[pl.ds(0, 2)])
    loads[4].wait()
    dp = mm(pw[:, 0:equart], cf[0].reshape(equart, npool), NN)
    for i in range(1, ntp):
        dp = dp + mm(pw[:, i * equart : (i + 1) * equart], cf[i].reshape(equart, npool), NN)
    dp = (dp / counts_row).astype(jnp.bfloat16)
    d0[...] = dp.reshape(groups, frows, npool)

    def along(size, mine, target, pairs):
        for src, dst, kind in pairs:
            pltpu.make_async_copy(src(mine), dst, recv.at[kind]).start()
        for i in range(1, size):
            to = lax.rem(mine + i, size)
            for src, dst, kind in pairs:
                remote(src(to), dst, kind, tok=target(to)).start()

    along(
        ny, myy, lambda y: y * plane + myp,
        [(lambda y: d0.at[pl.ds(2 * y, 2)], d1.at[myy], DY), (lambda y: pmap, m1.at[myy], MY)],
    )

    send_planes(order[ny // 2 :])

    for i in range(NX):
        dx = lax.rem(mex + i, NX)
        if i == 0:
            pltpu.make_async_copy(cf.at[:, :, dx], cx.at[mex], recv.at[COTX]).start()
        else:
            pltpu.make_async_remote_copy(
                src_ref=cf.at[:, :, dx], dst_ref=cx.at[mex], send_sem=send.at[COTX], recv_sem=recv.at[COTX],
                device_id={"tok": mehi * NX + dx}, device_id_type=MESH,
            ).start()

    def across(ref, bit, s, dims):
        w = section_matrix(mixw, s)
        stride = 1 << bit
        half = nt // 2
        run = min(16, half)

        for c in range(half // run):
            if stride >= run:
                p = c * run
                lo = (p // stride) * (2 * stride) + p % stride
                a = ref[lo : lo + run].reshape(run * frows, BLK)
                b = ref[lo + stride : lo + stride + run].reshape(run * frows, BLK)
                out = mm(jnp.concatenate([a, b], axis=1), w, dims).astype(jnp.bfloat16)
                ref[lo : lo + run] = out[:, :BLK].reshape(run, frows, BLK)
                ref[lo + stride : lo + stride + run] = out[:, BLK:].reshape(run, frows, BLK)
            else:
                base = c * 2 * run
                v = ref[base : base + 2 * run].reshape(run // stride, 2, stride, frows, BLK)
                a = v[:, 0].reshape(run * frows, BLK)
                b = v[:, 1].reshape(run * frows, BLK)
                out = mm(jnp.concatenate([a, b], axis=1), w, dims).astype(jnp.bfloat16)
                a = out[:, :BLK].reshape(run // stride, 1, stride, frows, BLK)
                b = out[:, BLK:].reshape(run // stride, 1, stride, frows, BLK)
                ref[base : base + 2 * run] = jnp.concatenate([a, b], axis=1).reshape(2 * run, frows, BLK)

    bits = nt.bit_length() - 1
    wait_bytes(recv.at[DY], d1)
    wait_bytes(recv.at[MY], m1)
    along(
        nz, myz, lambda z: myy * plane + z * NX + mex,
        [
            (lambda z: d1.at[:, lax.div(z, 2)], d2.at[myz], DZ),
            (lambda z: m1.at[:, pl.ds(lax.rem(z, 2) * NX, NX)], m2.at[myz], MZ),
        ],
    )

    loads[5].wait()
    wait_bytes(recv.at[F_IN], yt)
    for bit in range(bits):
        across(yt, bit, 3 + bit, NT)

    wait_bytes(recv.at[DZ], d2)
    wait_bytes(recv.at[MZ], m2)
    for i in range(1, NX):
        x = lax.rem(mex + i, NX)
        remote(d2, d3.at[mex], DX + i, tok=mehi * NX + x).start()
        remote(m2.at[:, :, x], m3.at[mex], MX + i, tok=mehi * NX + x).start()
    exchange(F_OUT, yt, xr)

    rank = lax.broadcasted_iota(jnp.int32, (npool, BLK), 0)
    for i in range(NX):
        x = lax.rem(mex - i + NX, NX)
        if i > 0:
            wait_bytes(recv.at[DX + i], d2)
            wait_bytes(recv.at[MX + i], m3.at[0])
        for z in range(nz):
            for y in range(ny):
                t = (y * nz + z) * NX + x
                row = (m2[z, y, mex] if i == 0 else m3[x, z, y]) - t * npool
                hit = rank == jnp.broadcast_to(row, (npool, BLK))
                rows_in = d2[z, y] if i == 0 else d3[x, z, y]
                ut[t] = mm(rows_in, jnp.where(hit, 1.0, 0.0).astype(jnp.bfloat16), NN).astype(jnp.bfloat16)
    for bit in reversed(range(bits)):
        across(ut, bit, 3 + bit, NN)
    exchange(B_OUT, ut, vt, 0, nt // 2)

    wait_bytes(recv.at[F_OUT], xr)
    total = mm(onehot[:, 0:BLK], load_block(xr, 0), NT)
    for j in range(1, blocks):
        total = total + mm(onehot[:, j * BLK : (j + 1) * BLK], load_block(xr, j), NT)
    pool[...] = (total / counts_col).astype(jnp.bfloat16)
    for i in range(NX):
        dx = lax.rem(mex + i, NX)
        if i == 0:
            pltpu.make_async_copy(pool, px.at[mex], recv.at[POOLX]).start()
        else:
            pltpu.make_async_remote_copy(
                src_ref=pool, dst_ref=px.at[mex], send_sem=send.at[POOLX], recv_sem=recv.at[POOLX],
                device_id={"tok": mehi * NX + dx}, device_id_type=MESH,
            ).start()
    for i in range(ntp):
        ps[i] = mm(pool[...], pw[:, i * equart : (i + 1) * equart], NN).astype(jnp.bfloat16)
    remote(ps.at[mate], pr.at[0], PROJ, tp=mate).start()
    remote(ps.at[diagonal], pr.at[1], PROJ, tp=mate).start()
    exchange(B_OUT, ut, vt, nt // 2, nt)

    wait_bytes(recv.at[PROJ], pr.at[pl.ds(0, 2)])
    far = ps[across_z].astype(jnp.float32) + pr[1].astype(jnp.float32)
    pr[2] = far.astype(jnp.bfloat16)
    remote(pr.at[2], pr.at[3], PROJZ, tp=across_z).start()

    wait_bytes(recv.at[COTX], cx)
    wait_bytes(recv.at[POOLX], px)
    for q in range(ntp):
        n = others // ntp
        part = mm(cx[0, q].reshape(n * erows, npool), px[0], NN)
        for i in range(1, NX):
            part = part + mm(cx[i, q].reshape(n * erows, npool), px[i], NN)
        cs[q * n : (q + 1) * n] = part.astype(jnp.bfloat16).reshape(n, erows, feats)

    def give(i, c):
        b = lax.rem(mehi + i, others)
        remote(cs.at[b], cr.at[mehi], GRAD, tok=b * NX + mex).start()
        return c

    pltpu.make_async_copy(cs.at[mehi], cr.at[mehi], recv.at[GRAD]).start()
    lax.fori_loop(1, others, give, 0)

    wait_bytes(recv.at[B_OUT], vt)
    for bit in (2, 1):
        w = section_matrix(mixw, bit)
        for lo, hi in local_pairs(bit):
            pair = jnp.concatenate([load_block(vt, lo), load_block(vt, hi)], axis=1)
            out = mm(pair, w, NN).astype(jnp.bfloat16)
            store_block(vt, lo, out[:, :BLK])
            store_block(vt, hi, out[:, BLK:])
    w = section_matrix(mixw, 0)
    for lo, hi in local_pairs(0):
        pair = jnp.concatenate([load_block(vt, lo), load_block(vt, hi)], axis=1)
        token_grad[lo * BLK : (hi + 1) * BLK] = mm(pair, w, NN).T.astype(jnp.bfloat16)

    wait_bytes(recv.at[PROJZ], pr.at[3])
    near = ps[mytp].astype(jnp.float32) + pr[0].astype(jnp.float32)
    projected[...] = (near + pr[3].astype(jnp.float32)).astype(jnp.bfloat16)

    wait_bytes(recv.at[GRAD], cr)
    proj_grad[...] = jnp.sum(cr[...].astype(jnp.float32), axis=0) * (1.0 / math.sqrt(npool * nt))

    for kind, ref in ((F_IN, yt), (F_OUT, xr), (B_OUT, vt)):
        wait_bytes(send.at[kind], ref.at[pl.ds(0, nt - 1)])
    for i in range(1, NX):
        wait_bytes(send.at[DX + i], d2)
        wait_bytes(send.at[MX + i], m3.at[0])
    for kind, ref in ((DY, d1), (DZ, d2), (MY, m1), (MZ, m2)):
        wait_bytes(send.at[kind], ref.at[pl.ds(0, ref.shape[0] - 1)])
    wait_bytes(send.at[COT], cf.at[pl.ds(0, 2)])
    wait_bytes(send.at[COTZ], cf.at[0])
    wait_bytes(send.at[PROJ], pr.at[pl.ds(0, 2)])
    wait_bytes(send.at[PROJZ], pr.at[0])
    wait_bytes(send.at[COTX], cx.at[pl.ds(0, NX - 1)])
    wait_bytes(send.at[POOLX], px.at[pl.ds(0, NX - 1)])
    wait_bytes(send.at[GRAD], cr.at[pl.ds(0, others - 1)])


def shards(nt, ntp, ny, tokens, mixw, pw, pool_map, cot):
    rows, feats = tokens.shape
    blocks = rows // BLK
    groups = nt // blocks
    frows = feats // groups
    nz = nt // (ny * NX)
    npool, equart = cot.shape
    others = nt // NX
    erows = equart // others
    share = equart // (NX * erows)
    bf = jnp.bfloat16
    tiles = pltpu.VMEM((nt, frows, BLK), bf)
    vmem = pl.BlockSpec(memory_space=pltpu.VMEM)
    return pl.pallas_call(
        functools.partial(kernel, nt, ntp, ny),
        out_shape=(
            jax.ShapeDtypeStruct((npool, equart), bf),
            jax.ShapeDtypeStruct((rows, feats), bf),
            jax.ShapeDtypeStruct((erows, feats), jnp.float32),
        ),
        in_specs=[pl.BlockSpec(memory_space=pltpu.HBM)] * 5,
        out_specs=(vmem,) * 3,
        scratch_shapes=[
            pltpu.VMEM((rows, feats), bf),
            pltpu.VMEM(mixw.shape, bf),
            pltpu.VMEM(pw.shape, bf),
            pltpu.VMEM((blocks, 1, BLK), jnp.int32),
            pltpu.VMEM((npool, equart), bf),
            pltpu.SemaphoreType.DMA((6,)),
            tiles, tiles, tiles, tiles, tiles,
            pltpu.VMEM((groups, frows, npool), bf),
            pltpu.VMEM((ny, 2, frows, npool), bf),
            pltpu.VMEM((nz, ny, frows, npool), bf),
            pltpu.VMEM((NX, nz, ny, frows, npool), bf),
            pltpu.VMEM((ny, blocks, 1, BLK), jnp.int32),
            pltpu.VMEM((nz, ny, NX, 1, BLK), jnp.int32),
            pltpu.VMEM((NX, nz, ny, 1, BLK), jnp.int32),
            pltpu.VMEM((npool, rows), bf),
            pltpu.VMEM((ntp, share, NX, erows, npool), bf),
            pltpu.VMEM((NX, ntp, share, erows, npool), bf),
            pltpu.VMEM((npool, feats), bf),
            pltpu.VMEM((NX, npool, feats), bf),
            pltpu.VMEM((ntp, npool, equart), bf),
            pltpu.VMEM((ntp, npool, equart), bf),
            pltpu.VMEM((others, erows, feats), bf),
            pltpu.VMEM((others, erows, feats), bf),
            pltpu.SemaphoreType.DMA((22,)),
            pltpu.SemaphoreType.DMA((22,)),
            pltpu.SemaphoreType.REGULAR((ny,)),
        ],
        compiler_params=pltpu.CompilerParams(collective_id=0, has_side_effects=True, vmem_limit_bytes=18 << 20),
    )(*[pltpu.with_memory_space_constraint(a, pltpu.HBM) for a in (tokens, mixw, pw, pool_map.reshape(blocks, 1, BLK), cot)])


def solution(mesh):
    nt, ntp = mesh.shape["tok"], mesh.shape["tp"]
    return jax.shard_map(
        functools.partial(shards, nt, ntp, nt // 16),
        mesh=mesh,
        in_specs=(P("tok", "tp"), P(), P("tp", None), P("tok"), P("tok", "tp")),
        out_specs=(P("tok", "tp"), P("tok", "tp"), P("tok", "tp")),
        check_vma=False,
    )
```

```python
import functools
import math

import jax
import jax.numpy as jnp
from jax import lax
from jax.experimental import pallas as pl
from jax.experimental.pallas import tpu as pltpu
from jax.sharding import PartitionSpec as P

MESH = pl.DeviceIdType.MESH
BLK = 128
NX = 4
NN = (((1,), (0,)), ((), ()))
NT = (((1,), (1,)), ((), ()))
F_IN, F_OUT, B_OUT, COT, COTX, POOLX, PROJ, GRAD, COTZ, PROJZ, DY, DZ, MY, MZ = range(14)
DX, MX = 14, 18


def mm(a, b, dims):
    return lax.dot_general(a, b, dims, preferred_element_type=jnp.float32)


def section_matrix(mixw, s):
    top = jnp.concatenate([mixw[s, 0, 0], mixw[s, 0, 1]], axis=1)
    low = jnp.concatenate([mixw[s, 1, 0], mixw[s, 1, 1]], axis=1)
    return jnp.concatenate([top, low], axis=0)


def wait_bytes(sem, ref):
    pltpu.make_async_copy(ref, ref, sem).wait()


def kernel(
    nt, ntp, ny, tokens_h, mixw_h, pw_h, pmap_h, cot_h, projected, token_grad, proj_grad,
    tokens, mixw, pw, pmap, cot, load, xs, yt, xr, ut, vt, d0, d1, d2, d3, m1, m2, m3, onehot, cf, cx, pool, px, ps, pr, cs, cr, send, recv, ready,
):
    me = lax.axis_index("tok")
    mytp = lax.axis_index("tp")
    rows, feats = tokens.shape
    blocks = rows // BLK
    groups = nt // blocks
    frows = feats // groups
    npool = cot.shape[0]
    equart = cot.shape[1]
    others = nt // NX
    erows = proj_grad.shape[0]
    mex, mehi = lax.rem(me, NX), lax.div(me, NX)
    nz = nt // (ny * NX)
    myz = lax.rem(mehi, nz)

    loads = [
        pltpu.make_async_copy(cot_h, cot, load.at[0]),
        pltpu.make_async_copy(tokens_h, tokens, load.at[1]),
        pltpu.make_async_copy(mixw_h.at[0:3], mixw.at[0:3], load.at[2]),
        pltpu.make_async_copy(pmap_h, pmap, load.at[3]),
        pltpu.make_async_copy(pw_h, pw, load.at[4]),
        pltpu.make_async_copy(mixw_h.at[3:], mixw.at[3:], load.at[5]),
    ]
    for one in loads:
        one.start()

    barrier = pltpu.get_barrier_semaphore()
    plane = nt // ny
    myy, myp = lax.div(me, plane), lax.rem(me, plane)

    def greet(i, c):
        d = myy * plane + lax.rem(myp + i, plane)
        pl.semaphore_signal(barrier, inc=1, device_id={"tok": d}, device_id_type=MESH)
        return c

    def greet_line(i, c):
        d = lax.rem(myy + i, ny) * plane + myp
        pl.semaphore_signal(barrier, inc=1, device_id={"tok": d}, device_id_type=MESH)
        return c

    lax.fori_loop(1, plane, greet, 0)
    lax.fori_loop(1, ny, greet_line, 0)
    for i in range(1, ntp):
        pl.semaphore_signal(barrier, inc=1, device_id={"tp": lax.rem(mytp + i, ntp)}, device_id_type=MESH)

    def exchange(kind, src, dst, first=0, last=nt):
        def one(i, c):
            d = lax.rem(me + i, nt)
            pltpu.make_async_remote_copy(
                src_ref=src.at[d], dst_ref=dst.at[me], send_sem=send.at[kind], recv_sem=recv.at[kind],
                device_id={"tok": d}, device_id_type=MESH,
            ).start()
            return c

        if first == 0:
            pltpu.make_async_copy(src.at[me], dst.at[me], recv.at[kind]).start()
        lax.fori_loop(max(first, 1), last, one, 0)

    def remote(src, dst, kind, **to):
        return pltpu.make_async_remote_copy(
            src_ref=src, dst_ref=dst, send_sem=send.at[kind], recv_sem=recv.at[kind],
            device_id=to, device_id_type=MESH,
        )

    def load_block(ref, j):
        parts = [ref[g * blocks + j] for g in range(groups)]
        return jnp.concatenate(parts, axis=0) if groups > 1 else parts[0]

    def store_block(ref, j, value):
        for g in range(groups):
            ref[g * blocks + j] = value[g * frows : (g + 1) * frows]

    def local_pairs(bit):
        return [(j, j | (1 << bit)) for j in range(blocks) if not j & (1 << bit)]

    loads[0].wait()
    cf[mytp] = cot[...].astype(jnp.float32).T.astype(jnp.bfloat16).reshape(cf.shape[1:])

    loads[1].wait()
    loads[2].wait()
    w = section_matrix(mixw, 0)
    for lo, hi in local_pairs(0):
        out = mm(w, tokens[lo * BLK : (hi + 1) * BLK], NN).T.astype(jnp.bfloat16)
        store_block(xs, lo, out[:, :BLK])
        store_block(xs, hi, out[:, BLK:])
    for bit in (1, 2):
        w = section_matrix(mixw, bit)
        for lo, hi in local_pairs(bit):
            pair = jnp.concatenate([load_block(xs, lo), load_block(xs, hi)], axis=1)
            out = mm(pair, w, NT).astype(jnp.bfloat16)
            store_block(xs, lo, out[:, :BLK])
            store_block(xs, hi, out[:, BLK:])

    pl.semaphore_wait(barrier, plane - 1 + ny - 1 + ntp - 1)

    def announce(i, c):
        d = lax.rem(myy + i, ny) * plane + myp
        pl.semaphore_signal(ready.at[myy], inc=1, device_id={"tok": d}, device_id_type=MESH)
        return c

    lax.fori_loop(1, ny, announce, 0)
    mate, across_z, diagonal = mytp ^ 1, mytp ^ 2, mytp ^ 3
    remote(cf.at[mytp], cf.at[mytp], COTZ, tp=across_z).start()
    remote(cf.at[mytp], cf.at[mytp], COT, tp=mate).start()

    pltpu.make_async_copy(xs.at[me], yt.at[me], recv.at[F_IN]).start()
    order = [0] + sorted(range(1, ny), key=lambda step: -min(step, ny - step))

    def send_planes(steps):
        for step in steps:
            y = lax.rem(myy + step, ny)
            if step > 0:
                pl.semaphore_wait(ready.at[y], 1)

            def to_plane(i, c, y=y):
                d = y * plane + lax.rem(myp + i, plane)
                remote(xs.at[d], yt.at[me], F_IN, tok=d).start()
                return c

            lax.fori_loop(0 if step > 0 else 1, plane, to_plane, 0)

    send_planes(order[: ny // 2])

    loads[3].wait()
    pid = lax.broadcasted_iota(jnp.int32, (npool, BLK), 0) + me * npool
    for j in range(blocks):
        hit = pid == jnp.broadcast_to(pmap[j], (npool, BLK))
        onehot[:, j * BLK : (j + 1) * BLK] = jnp.where(hit, 1.0, 0.0).astype(jnp.bfloat16)
    ones = jnp.ones((8, blocks * BLK), jnp.bfloat16)
    counts_row = mm(ones, onehot[...], NT)[0:1]
    counts_col = jnp.sum(onehot[...].astype(jnp.float32), axis=1, keepdims=True)

    wait_bytes(recv.at[COTZ], cf.at[0])
    remote(cf.at[across_z], cf.at[across_z], COT, tp=mate).start()
    wait_bytes(recv.at[COT], cf.at[pl.ds(0, 2)])
    loads[4].wait()
    dp = mm(pw[:, 0:equart], cf[0].reshape(equart, npool), NN)
    for i in range(1, ntp):
        dp = dp + mm(pw[:, i * equart : (i + 1) * equart], cf[i].reshape(equart, npool), NN)
    dp = (dp / counts_row).astype(jnp.bfloat16)
    d0[...] = dp.reshape(groups, frows, npool)

    def along(size, mine, target, pairs):
        for src, dst, kind in pairs:
            pltpu.make_async_copy(src(mine), dst, recv.at[kind]).start()
        for i in range(1, size):
            to = lax.rem(mine + i, size)
            for src, dst, kind in pairs:
                remote(src(to), dst, kind, tok=target(to)).start()

    along(
        ny, myy, lambda y: y * plane + myp,
        [(lambda y: d0.at[pl.ds(2 * y, 2)], d1.at[myy], DY), (lambda y: pmap, m1.at[myy], MY)],
    )

    send_planes(order[ny // 2 :])

    for i in range(NX):
        dx = lax.rem(mex + i, NX)
        if i == 0:
            pltpu.make_async_copy(cf.at[:, :, dx], cx.at[mex], recv.at[COTX]).start()
        else:
            pltpu.make_async_remote_copy(
                src_ref=cf.at[:, :, dx], dst_ref=cx.at[mex], send_sem=send.at[COTX], recv_sem=recv.at[COTX],
                device_id={"tok": mehi * NX + dx}, device_id_type=MESH,
            ).start()

    def across(ref, bit, s, dims):
        w = section_matrix(mixw, s)
        stride = 1 << bit
        half = nt // 2
        run = min(16, half)

        for c in range(half // run):
            if stride >= run:
                p = c * run
                lo = (p // stride) * (2 * stride) + p % stride
                a = ref[lo : lo + run].reshape(run * frows, BLK)
                b = ref[lo + stride : lo + stride + run].reshape(run * frows, BLK)
                out = mm(jnp.concatenate([a, b], axis=1), w, dims).astype(jnp.bfloat16)
                ref[lo : lo + run] = out[:, :BLK].reshape(run, frows, BLK)
                ref[lo + stride : lo + stride + run] = out[:, BLK:].reshape(run, frows, BLK)
            else:
                base = c * 2 * run
                v = ref[base : base + 2 * run].reshape(run // stride, 2, stride, frows, BLK)
                a = v[:, 0].reshape(run * frows, BLK)
                b = v[:, 1].reshape(run * frows, BLK)
                out = mm(jnp.concatenate([a, b], axis=1), w, dims).astype(jnp.bfloat16)
                a = out[:, :BLK].reshape(run // stride, 1, stride, frows, BLK)
                b = out[:, BLK:].reshape(run // stride, 1, stride, frows, BLK)
                ref[base : base + 2 * run] = jnp.concatenate([a, b], axis=1).reshape(2 * run, frows, BLK)

    bits = nt.bit_length() - 1
    wait_bytes(recv.at[DY], d1)
    wait_bytes(recv.at[MY], m1)
    along(
        nz, myz, lambda z: myy * plane + z * NX + mex,
        [
            (lambda z: d1.at[:, lax.div(z, 2)], d2.at[myz], DZ),
            (lambda z: m1.at[:, pl.ds(lax.rem(z, 2) * NX, NX)], m2.at[myz], MZ),
        ],
    )

    loads[5].wait()
    wait_bytes(recv.at[F_IN], yt)
    for bit in range(bits):
        across(yt, bit, 3 + bit, NT)

    exchange(F_OUT, yt, xr, 0, nt // 2)

    wait_bytes(recv.at[DZ], d2)
    wait_bytes(recv.at[MZ], m2)
    for i in range(1, NX):
        x = lax.rem(mex + i, NX)
        remote(d2, d3.at[mex], DX + i, tok=mehi * NX + x).start()
        remote(m2.at[:, :, x], m3.at[mex], MX + i, tok=mehi * NX + x).start()
    exchange(F_OUT, yt, xr, nt // 2, nt)

    rank = lax.broadcasted_iota(jnp.int32, (npool, BLK), 0)
    for i in range(NX):
        x = lax.rem(mex - i + NX, NX)
        if i > 0:
            wait_bytes(recv.at[DX + i], d2)
            wait_bytes(recv.at[MX + i], m3.at[0])
        for z in range(nz):
            for y in range(ny):
                t = (y * nz + z) * NX + x
                row = (m2[z, y, mex] if i == 0 else m3[x, z, y]) - t * npool
                hit = rank == jnp.broadcast_to(row, (npool, BLK))
                rows_in = d2[z, y] if i == 0 else d3[x, z, y]
                ut[t] = mm(rows_in, jnp.where(hit, 1.0, 0.0).astype(jnp.bfloat16), NN).astype(jnp.bfloat16)
    for bit in reversed(range(bits)):
        across(ut, bit, 3 + bit, NN)
    exchange(B_OUT, ut, vt, 0, nt // 2)

    wait_bytes(recv.at[F_OUT], xr)
    total = mm(onehot[:, 0:BLK], load_block(xr, 0), NT)
    for j in range(1, blocks):
        total = total + mm(onehot[:, j * BLK : (j + 1) * BLK], load_block(xr, j), NT)
    pool[...] = (total / counts_col).astype(jnp.bfloat16)
    for i in range(NX):
        dx = lax.rem(mex + i, NX)
        if i == 0:
            pltpu.make_async_copy(pool, px.at[mex], recv.at[POOLX]).start()
        else:
            pltpu.make_async_remote_copy(
                src_ref=pool, dst_ref=px.at[mex], send_sem=send.at[POOLX], recv_sem=recv.at[POOLX],
                device_id={"tok": mehi * NX + dx}, device_id_type=MESH,
            ).start()
    for i in range(ntp):
        ps[i] = mm(pool[...], pw[:, i * equart : (i + 1) * equart], NN).astype(jnp.bfloat16)
    remote(ps.at[mate], pr.at[0], PROJ, tp=mate).start()
    remote(ps.at[diagonal], pr.at[1], PROJ, tp=mate).start()
    exchange(B_OUT, ut, vt, nt // 2, nt)

    wait_bytes(recv.at[PROJ], pr.at[pl.ds(0, 2)])
    far = ps[across_z].astype(jnp.float32) + pr[1].astype(jnp.float32)
    pr[2] = far.astype(jnp.bfloat16)
    remote(pr.at[2], pr.at[3], PROJZ, tp=across_z).start()

    wait_bytes(recv.at[COTX], cx)
    wait_bytes(recv.at[POOLX], px)
    for q in range(ntp):
        n = others // ntp
        part = mm(cx[0, q].reshape(n * erows, npool), px[0], NN)
        for i in range(1, NX):
            part = part + mm(cx[i, q].reshape(n * erows, npool), px[i], NN)
        cs[q * n : (q + 1) * n] = part.astype(jnp.bfloat16).reshape(n, erows, feats)

    def give(i, c):
        b = lax.rem(mehi + i, others)
        remote(cs.at[b], cr.at[mehi], GRAD, tok=b * NX + mex).start()
        return c

    pltpu.make_async_copy(cs.at[mehi], cr.at[mehi], recv.at[GRAD]).start()
    lax.fori_loop(1, others, give, 0)

    wait_bytes(recv.at[B_OUT], vt)
    for bit in (2, 1):
        w = section_matrix(mixw, bit)
        for lo, hi in local_pairs(bit):
            pair = jnp.concatenate([load_block(vt, lo), load_block(vt, hi)], axis=1)
            out = mm(pair, w, NN).astype(jnp.bfloat16)
            store_block(vt, lo, out[:, :BLK])
            store_block(vt, hi, out[:, BLK:])
    w = section_matrix(mixw, 0)
    for lo, hi in local_pairs(0):
        pair = jnp.concatenate([load_block(vt, lo), load_block(vt, hi)], axis=1)
        token_grad[lo * BLK : (hi + 1) * BLK] = mm(pair, w, NN).T.astype(jnp.bfloat16)

    wait_bytes(recv.at[PROJZ], pr.at[3])
    near = ps[mytp].astype(jnp.float32) + pr[0].astype(jnp.float32)
    projected[...] = (near + pr[3].astype(jnp.float32)).astype(jnp.bfloat16)

    wait_bytes(recv.at[GRAD], cr)
    proj_grad[...] = jnp.sum(cr[...].astype(jnp.float32), axis=0) * (1.0 / math.sqrt(npool * nt))

    for kind, ref in ((F_IN, yt), (F_OUT, xr), (B_OUT, vt)):
        wait_bytes(send.at[kind], ref.at[pl.ds(0, nt - 1)])
    for i in range(1, NX):
        wait_bytes(send.at[DX + i], d2)
        wait_bytes(send.at[MX + i], m3.at[0])
    for kind, ref in ((DY, d1), (DZ, d2), (MY, m1), (MZ, m2)):
        wait_bytes(send.at[kind], ref.at[pl.ds(0, ref.shape[0] - 1)])
    wait_bytes(send.at[COT], cf.at[pl.ds(0, 2)])
    wait_bytes(send.at[COTZ], cf.at[0])
    wait_bytes(send.at[PROJ], pr.at[pl.ds(0, 2)])
    wait_bytes(send.at[PROJZ], pr.at[0])
    wait_bytes(send.at[COTX], cx.at[pl.ds(0, NX - 1)])
    wait_bytes(send.at[POOLX], px.at[pl.ds(0, NX - 1)])
    wait_bytes(send.at[GRAD], cr.at[pl.ds(0, others - 1)])


def shards(nt, ntp, ny, tokens, mixw, pw, pool_map, cot):
    rows, feats = tokens.shape
    blocks = rows // BLK
    groups = nt // blocks
    frows = feats // groups
    nz = nt // (ny * NX)
    npool, equart = cot.shape
    others = nt // NX
    erows = equart // others
    share = equart // (NX * erows)
    bf = jnp.bfloat16
    tiles = pltpu.VMEM((nt, frows, BLK), bf)
    vmem = pl.BlockSpec(memory_space=pltpu.VMEM)
    return pl.pallas_call(
        functools.partial(kernel, nt, ntp, ny),
        out_shape=(
            jax.ShapeDtypeStruct((npool, equart), bf),
            jax.ShapeDtypeStruct((rows, feats), bf),
            jax.ShapeDtypeStruct((erows, feats), jnp.float32),
        ),
        in_specs=[pl.BlockSpec(memory_space=pltpu.HBM)] * 5,
        out_specs=(vmem,) * 3,
        scratch_shapes=[
            pltpu.VMEM((rows, feats), bf),
            pltpu.VMEM(mixw.shape, bf),
            pltpu.VMEM(pw.shape, bf),
            pltpu.VMEM((blocks, 1, BLK), jnp.int32),
            pltpu.VMEM((npool, equart), bf),
            pltpu.SemaphoreType.DMA((6,)),
            tiles, tiles, tiles, tiles, tiles,
            pltpu.VMEM((groups, frows, npool), bf),
            pltpu.VMEM((ny, 2, frows, npool), bf),
            pltpu.VMEM((nz, ny, frows, npool), bf),
            pltpu.VMEM((NX, nz, ny, frows, npool), bf),
            pltpu.VMEM((ny, blocks, 1, BLK), jnp.int32),
            pltpu.VMEM((nz, ny, NX, 1, BLK), jnp.int32),
            pltpu.VMEM((NX, nz, ny, 1, BLK), jnp.int32),
            pltpu.VMEM((npool, rows), bf),
            pltpu.VMEM((ntp, share, NX, erows, npool), bf),
            pltpu.VMEM((NX, ntp, share, erows, npool), bf),
            pltpu.VMEM((npool, feats), bf),
            pltpu.VMEM((NX, npool, feats), bf),
            pltpu.VMEM((ntp, npool, equart), bf),
            pltpu.VMEM((ntp, npool, equart), bf),
            pltpu.VMEM((others, erows, feats), bf),
            pltpu.VMEM((others, erows, feats), bf),
            pltpu.SemaphoreType.DMA((22,)),
            pltpu.SemaphoreType.DMA((22,)),
            pltpu.SemaphoreType.REGULAR((ny,)),
        ],
        compiler_params=pltpu.CompilerParams(collective_id=0, has_side_effects=True, vmem_limit_bytes=18 << 20),
    )(*[pltpu.with_memory_space_constraint(a, pltpu.HBM) for a in (tokens, mixw, pw, pool_map.reshape(blocks, 1, BLK), cot)])


def solution(mesh):
    nt, ntp = mesh.shape["tok"], mesh.shape["tp"]
    return jax.shard_map(
        functools.partial(shards, nt, ntp, nt // 16),
        mesh=mesh,
        in_specs=(P("tok", "tp"), P(), P("tp", None), P("tok"), P("tok", "tp")),
        out_specs=(P("tok", "tp"), P("tok", "tp"), P("tok", "tp")),
        check_vma=False,
    )
```
